256 devices in a mesh: tm: 16 (over z, core), block: 16 (over x, y).
Axes of the slice: x: 4, y: 4, z: 8, core: 2. Of those that a mesh axis runs over, the one named last changes fastest.
Arguments:
- state: float32 [16, 4, 256, 2048], P('tm', None, None, 'block'), may hold values from -6 to 6
- far_field: float32 [16, 4, 2048], P('tm', None, 'block'), may hold values from -6 to 6
- face_index: int32 [16, 2048], P('tm', 'block'), may hold values from 0 to 1023, as said below
- face_weight: float32 [16, 4, 2048], P('tm', None, 'block'), may hold values from 0.05 to 0.45
- mean_flow: float32 [2, 2], replicated, may hold values from -0.6 to 0.6
Outputs:
- new_state: float32 [16, 4, 256, 2048], P('tm', None, None, 'block')
The draws below stay inside these ranges and needn't reach their ends.
Inputs may be any that keep to these rules, and one draw needn't show every extreme that they name: `face_index`: each face's index points into the opposite row's 8 * 128 interface faces laid end to end; the 4 faces read wrap around that cycle. At each level, the faces of one blade row take distinct first indices, every face of the opposite row exactly once.
All inputs are finite; a program needn't handle non-finite values.
Results may differ from the reference program's by a relative error of at most 0.00016.
Values sent between devices are 32-bit elements; how exact they have to be, the bound alone decides.
No kernel may reach another device: no remote copies, remote signals or barrier semaphores. Data moves between devices by JAX's collectives and lax.ppermute only.
A program may use at most 64 MiB of HBM per device.

```python
import jax
import jax.numpy as jnp
from jax import lax

NT = 16
NI = 256
NJ = 128
K = 4
BLOCKS = 16
HALF = 8


def draw_face_index(key, part):
    base = jax.random.fold_in(key, 7)
    cycle_size = HALF * NJ
    level_keys = jax.random.split(base, NT * 2)
    orders = jax.vmap(lambda single: jax.random.permutation(single, cycle_size))(level_keys)
    column = jnp.arange(BLOCKS * NJ)
    block_number = column // NJ
    side = block_number // HALF
    place = block_number % HALF * NJ + column % NJ
    flat = orders.reshape(NT, 2 * cycle_size)
    return jnp.take(flat, side * cycle_size + place, axis=1).astype(jnp.int32)


def block_levels(stream_key, shape, cuts, smallest, top_value):
    level = 1.0
    for axis_at, blocks in cuts:
        draws = jax.random.uniform(jax.random.fold_in(jax.random.fold_in(stream_key, 6), axis_at), (blocks,), jnp.float32, smallest / len(cuts), top_value / len(cuts))
        level = level * jnp.repeat(jnp.exp(draws), shape[axis_at] // blocks).reshape((-1,) + (1,) * (len(shape) - 1 - axis_at))
    return level


def centred(own_key, extent, deviation, limit, cuts=(), held_as=jnp.bfloat16):
    factor_of = block_levels(own_key, extent, cuts, -0.22, 0.18) if cuts else 1.0
    entries = jax.random.normal(own_key, extent, jnp.float32) * deviation * factor_of
    return jnp.minimum(jnp.maximum(entries, -limit), limit).astype(held_as)


def setup_inputs(seed: int = 0) -> dict:
    keys = jax.random.split(jax.random.key(seed), 6)
    state = centred(keys[0], (NT, 4, NI, BLOCKS * NJ), 1.0, 6.0, ((0, 16), (3, 16)), jnp.float32)
    far_field = centred(keys[1], (NT, 4, BLOCKS * NJ), 1.0, 6.0, ((0, 16), (2, 16)), jnp.float32)
    face_index = draw_face_index(jax.random.fold_in(keys[5], 71), 0)
    face_weight = jnp.clip(0.05 + 0.39999999 * jax.random.uniform(keys[3], (NT, K, BLOCKS * NJ), jnp.float32) ** block_levels(keys[3], (NT, K, BLOCKS * NJ), ((0, 16), (2, 16)), -0.2, 0.2), 0.05, 0.45)
    mean_flow = jnp.clip(jax.random.uniform(keys[4], (2, 2), jnp.float32, -0.6, 0.6), -0.6, 0.6)
    return {"state": state, "far_field": far_field, "face_index": face_index, "face_weight": face_weight, "mean_flow": mean_flow}


SECTION_FACTORS = (0.075, 0.05, 0.1125, 0.15, 0.3)
OMEGA = 1.0
DISSIPATION = 0.2


def derivative_matrix(count):
    index = jnp.arange(count)
    offsets = index[:, None] - index[None, :]
    angle = jnp.pi * offsets.astype(jnp.float32) / count
    parity_sign = 1.0 - 2.0 * (offsets % 2).astype(jnp.float32)
    safe_angle = jnp.where(offsets == 0, 0.5 * jnp.pi, angle)
    cotangent = jnp.cos(safe_angle) / jnp.sin(safe_angle)
    return jnp.where(offsets == 0, 0.0, 0.5 * parity_sign * cotangent).astype(jnp.float32)


def interpolate(faces, table, weight):
    cycle_size = faces.shape[2]
    total = jnp.zeros(faces.shape, jnp.float32)
    for offset in range(weight.shape[1]):
        source = ((table + offset) % cycle_size).astype(jnp.int32)
        picked = jnp.take_along_axis(faces, jnp.broadcast_to(source[:, None, :], faces.shape), axis=2)
        total = total + weight[:, offset][:, None, :] * picked
    return total


def residual(field, lower_ghost, upper_ghost, lower_col, upper_col, speed_u, speed_v):
    padded_i = jnp.concatenate([lower_ghost[:, :, None], field, upper_ghost[:, :, None]], axis=2)
    padded_j = jnp.concatenate([lower_col, field, upper_col], axis=3)
    diff_i = padded_i[:, :, 2:] - padded_i[:, :, :-2]
    diff_j = padded_j[..., 2:] - padded_j[..., :-2]
    laplace = (padded_i[:, :, 2:] - 2.0 * field + padded_i[:, :, :-2]) + (padded_j[..., 2:] - 2.0 * field + padded_j[..., :-2])
    flux_i = jnp.stack([speed_u * diff_i[:, 0] + diff_i[:, 1], speed_u * diff_i[:, 1] + diff_i[:, 3],
                        speed_u * diff_i[:, 2], speed_u * diff_i[:, 3] + diff_i[:, 1]], axis=1)
    flux_j = jnp.stack([speed_v * diff_j[:, 0] + diff_j[:, 2], speed_v * diff_j[:, 1],
                        speed_v * diff_j[:, 2] + diff_j[:, 3], speed_v * diff_j[:, 3] + diff_j[:, 2]], axis=1)
    return 0.5 * (flux_i + flux_j) - DISSIPATION * laplace


def reference(state, far_field, face_index, face_weight, mean_flow):
    half = BLOCKS // 2
    spectral = derivative_matrix(NT)
    far_rows = far_field.reshape(NT, 4, 2, half * NJ)
    tables = face_index.reshape(NT, 2, half * NJ)
    weights = face_weight.reshape(NT, K, 2, half * NJ)
    field = state
    for factor in SECTION_FACTORS:
        blocked = field.reshape(NT, 4, NI, 2, half * NJ)
        pieces = []
        for side in (0, 1):
            part = blocked[:, :, :, side]
            other = blocked[:, :, :, 1 - side]
            other_face = other[:, :, 0] if side == 0 else other[:, :, NI - 1]
            ghost = interpolate(other_face, tables[:, side], weights[:, :, side])
            far_side = far_rows[:, :, side]
            if side == 0:
                lower_ghost, upper_ghost = far_side, ghost
            else:
                lower_ghost, upper_ghost = ghost, far_side
            flux = residual(part, lower_ghost, upper_ghost, part[..., -1:], part[..., :1],
                            mean_flow[side, 0], mean_flow[side, 1])
            pieces.append(flux)
        flux_all = jnp.stack(pieces, axis=3).reshape(NT, 4, NI, BLOCKS * NJ)
        deriv = jnp.einsum('nm,mvij->nvij', spectral, field, precision=lax.Precision.HIGHEST)
        field = state - factor * (flux_all + OMEGA * deriv)
    return field
```

```python
import functools

import jax
import jax.numpy as jnp
import numpy as np
from jax import lax
from jax.experimental import pallas as pl
from jax.experimental.pallas import tpu as pltpu
from jax.sharding import PartitionSpec as P

SECTION_FACTORS = (0.075, 0.05, 0.1125, 0.15, 0.3)
OMEGA = 1.0
DISSIPATION = 0.2

NT = 16
NV = 4
CHUNK = 16
HALO = 5
LINES = CHUNK + 2 * HALO
W = 128
HALF = 8
BLOCKS = 16
NR = 112
BEFORE, AFTER, TABLE = 64, 84, 104
ZONE = 25
HALF_ZONE = 13
EDGE_PACKS = 7
VMEM = pl.BlockSpec(memory_space=pltpu.VMEM)
SMEM = pl.BlockSpec(memory_space=pltpu.SMEM)


def level_matrix():
    offsets = np.arange(NT)[:, None] - np.arange(NT)[None, :]
    angle = np.pi * offsets / NT
    safe = np.where(offsets == 0, 0.5 * np.pi, angle)
    cot = np.cos(safe) / np.sin(safe)
    matrix = np.where(offsets == 0, 0.0, 0.5 * (1.0 - 2.0 * (offsets % 2)) * cot)
    matrix = OMEGA * matrix + 4.0 * DISSIPATION * np.eye(NT)
    return np.kron(np.eye(NV), matrix).astype(np.float32)


def params(mib):
    return pltpu.CompilerParams(vmem_limit_bytes=mib << 20)


def place():
    return lax.axis_index("tm"), lax.axis_index("block")


def line_address(side, r, v):
    if r < 0:
        rotor, stator = BEFORE + v * HALO + r + HALO, AFTER + v * HALO - 1 - r
    elif r < CHUNK:
        rotor, stator = v * CHUNK + r, v * CHUNK + CHUNK - 1 - r
    else:
        rotor, stator = AFTER + v * HALO + r - CHUNK, BEFORE + v * HALO + 20 - r
    return jnp.where(side == 0, rotor, stator)


def pack_kernel(state, far, index, weight, out):
    _, block = place()
    side = block // HALF
    rotor = side == 0
    table = jnp.concatenate([index[...].astype(jnp.float32), weight[...], jnp.zeros((3, W), jnp.float32)], axis=0)
    for t in range(NT):
        chunk = jnp.where(rotor, t, NT - 1 - t)
        start = pl.multiple_of(chunk * CHUNK, CHUNK)
        low = pl.multiple_of(jnp.maximum(start - 8, 0), 8)
        high = pl.multiple_of(jnp.minimum(start + CHUNK, 248), 8)
        for v in range(NV):
            out[t, v * CHUNK : (v + 1) * CHUNK] = state[v, pl.ds(start, CHUNK)]
            before = state[v, pl.ds(low, 8)][3:8]
            after = state[v, pl.ds(high, 8)][0:5]
            if t == 0:
                ghost = jnp.broadcast_to(far[v : v + 1], (HALO, W))
                before = jnp.where(rotor, ghost, before)
                after = jnp.where(rotor, after, ghost)
            out[t, BEFORE + v * HALO : BEFORE + (v + 1) * HALO] = before
            out[t, AFTER + v * HALO : AFTER + (v + 1) * HALO] = after
        out[t, TABLE:NR] = table


def zone_kernel(lines, low, high, left, right):
    _, block = place()
    side = block // HALF
    for k in range(ZONE):
        if k < 20:
            address = line_address(side, CHUNK - 1 - k // NV, k % NV)
        else:
            address = TABLE + k - 20
        tile = lines[pl.ds(address, NT, stride=NR), :]
        if k < HALF_ZONE:
            low[k * NT : (k + 1) * NT] = tile
        else:
            high[(k - HALF_ZONE) * NT : (k - HALF_ZONE + 1) * NT] = tile
    high[(HALF_ZONE - 1) * NT :] = jnp.zeros((NT, W), jnp.float32)
    part = lax.broadcasted_iota(jnp.int32, (NT, W), 1) // 8
    for p in range(EDGE_PACKS):
        left_pack = jnp.zeros((NT, W), jnp.float32)
        right_pack = jnp.zeros((NT, W), jnp.float32)
        for k in range(16):
            m = p * 16 + k
            if m >= LINES * NV:
                break
            tile = lines[pl.ds(line_address(side, m // NV - HALO, m % NV), NT, stride=NR), :]
            moved = tile if k == 0 else pltpu.roll(tile, 8 * k, 1)
            left_pack = jnp.where(part == k, moved, left_pack)
            moved = tile if k == 15 else pltpu.roll(tile, 8 * k + 8, 1)
            right_pack = jnp.where(part == k, moved, right_pack)
        left[p * NT : (p + 1) * NT] = left_pack
        right[p * NT : (p + 1) * NT] = right_pack


def coefficients(flow, side):
    sign = jnp.where(side == 0, 0.5, -0.5)
    along = sign * flow[side, 0]
    across = 0.5 * flow[side, 1]
    return sign, along - DISSIPATION, -along - DISSIPATION, across - DISSIPATION, -across - DISSIPATION


def rates(coefs, up, down, nxt, prv, timed):
    sign, cu, cd, cn, cp = coefs
    plain = [timed[v] + (cu * up[v] + cd * down[v]) + (cn * nxt[v] + cp * prv[v]) for v in range(NV)]
    mixed = sign * (up[1] - down[1]) + 0.5 * (nxt[2] - prv[2])
    pressure_up = sign * (up[3] - down[3])
    pressure_next = 0.5 * (nxt[3] - prv[3])
    return [plain[0] + mixed, plain[1] + pressure_up, plain[2] + pressure_next, plain[3] + mixed]


def level_product(matrix, values):
    return jnp.dot(matrix, values, precision=lax.Precision.HIGHEST, preferred_element_type=jnp.float32)


def chain_kernel(low, high, matrix, flow, out, cur, ghosts):
    _, block = place()
    own_side, own = block // HALF, block % HALF
    lane = lax.broadcasted_iota(jnp.int32, (NT, W), 1)

    def tile(side, j, k):
        source, k = (low, k) if k < HALF_ZONE else (high, k - HALF_ZONE)
        return source[HALF * side + j, k * NT : (k + 1) * NT, :]

    def value(section, side, line, v, j):
        if section == 0:
            return tile(side, j, line * NV + v)
        return cur[section % 2, side, line, v, j]

    def interpolate(section, side, j):
        first = tile(side, j, 20).astype(jnp.int32)
        totals = [jnp.zeros((NT, W), jnp.float32)] * NV
        for k in range(4):
            source = (first + k) & (HALF * W - 1)
            within, which = source & (W - 1), source >> 7
            weight = tile(side, j, 21 + k)
            picked = [None] * NV
            for m in range(HALF):
                here = which == m
                for v in range(NV):
                    got = jnp.take_along_axis(value(section, 1 - side, 0, v, m), within, axis=1, mode="promise_in_bounds")
                    picked[v] = got if m == 0 else jnp.where(here, got, picked[v])
            totals = [totals[v] + weight * picked[v] for v in range(NV)]
        return totals

    for s in range(5):

        def ghost_step(step, _, s=s):
            side, j = step // HALF, step % HALF
            got = interpolate(s, side, j)
            for v in range(NV):
                ghosts[side, v, j] = got[v]
            return 0

        if s < 4:
            lax.fori_loop(0, 2 * HALF, ghost_step, 0)
            for v in range(NV):
                out[s, v, 0] = ghosts[own_side, v, own]
                after = ghosts[own_side, v, (own + 1) % HALF]
                before = ghosts[own_side, v, (own + HALF - 1) % HALF]
                out[s, v, 1] = jnp.where(lane < W // 2, after, before)
        else:
            got = interpolate(s, own_side, own)
            for v in range(NV):
                out[s, v, 0] = got[v]
                out[s, v, 1] = got[v]
            break

        def line_step(step, _, s=s):
            side, j = step // HALF, step % HALF
            after, before = (j + 1) % HALF, (j + HALF - 1) % HALF
            coefs = coefficients(flow, side)
            for line in range(4 - s):
                here = [value(s, side, line, v, j) for v in range(NV)]
                up = [ghosts[side, v, j] if line == 0 else value(s, side, line - 1, v, j) for v in range(NV)]
                down = [value(s, side, line + 1, v, j) for v in range(NV)]
                nxt = [
                    jnp.where(
                        lane == W - 1,
                        pltpu.roll(value(s, side, line, v, after), W - 1, 1),
                        pltpu.roll(here[v], W - 1, 1),
                    )
                    for v in range(NV)
                ]
                prv = [
                    jnp.where(
                        lane == 0, pltpu.roll(value(s, side, line, v, before), 1, 1), pltpu.roll(here[v], 1, 1)
                    )
                    for v in range(NV)
                ]
                product = level_product(matrix[...], jnp.concatenate(here, axis=0))
                timed = [product[v * NT : (v + 1) * NT] for v in range(NV)]
                rate = rates(coefs, up, down, nxt, prv, timed)
                for v in range(NV):
                    cur[(s + 1) % 2, side, line, v, j] = value(0, side, line, v, j) - SECTION_FACTORS[s] * rate[v]
            return 0

        lax.fori_loop(0, 2 * HALF, line_step, 0)


def bulk_kernel(lines, from_left, from_right, ghosts, matrix, flow, out, start, even, odd):
    t, block = place()
    side = block // HALF
    lane = lax.broadcasted_iota(jnp.int32, (NT, W), 1)
    for m in range(LINES * NV):
        r, v = m // NV - HALO, m % NV
        at = slice(v * NT, (v + 1) * NT)
        start[m // NV, at, :W] = lines[pl.ds(line_address(side, r, v), NT, stride=NR), :]
        p, k = m // 16, m % 16
        after = from_right[p * NT : (p + 1) * NT]
        after = after if k == 0 else pltpu.roll(after, W - 8 * k, 1)
        before = from_left[p * NT : (p + 1) * NT]
        before = before if k == 15 else pltpu.roll(before, 120 - 8 * k, 1)
        start[m // NV, at, W:] = jnp.where(lane < W // 2, after, before)
    coefs = coefficients(flow, side)
    for s in range(5):
        now = start if s == 0 else (even if s % 2 == 0 else odd)
        new = odd if s % 2 == 0 else even

        @pl.when(t == NT - 1)
        def _(now=now, s=s):
            for v in range(NV):
                at = slice(v * NT, (v + 1) * NT)
                now[HALO + CHUNK, at, :W] = ghosts[s, v, 0]
                now[HALO + CHUNK, at, W:] = ghosts[s, v, 1]

        if s > 0:

            @pl.when(t == 0)
            def _(now=now):
                now[HALO - 1] = start[HALO - 1]

        def line_step(i, _, now=now, new=new, s=s):
            here = now[i]
            split = lambda x: [x[v * NT : (v + 1) * NT] for v in range(NV)]
            nxt = pltpu.roll(here, 2 * W - 1, 1)
            prv = pltpu.roll(here, 1, 1)
            timed = level_product(matrix[...], here)
            rate = rates(coefs, split(now[i + 1]), split(now[i - 1]), split(nxt), split(prv), split(timed))
            base = split(start[i])
            for v in range(NV):
                result = base[v] - SECTION_FACTORS[s] * rate[v]
                if s < 4:
                    new[i, v * NT : (v + 1) * NT] = result
                else:
                    cell = jnp.where(side == 0, i - HALO, CHUNK - 1 + HALO - i)
                    out[pl.ds(v * CHUNK + cell, NT, stride=NV * CHUNK), :] = result[:, :W]
            return 0

        lax.fori_loop(s + 1, LINES - 1 - s, line_step, 0)


def unpack_kernel(shares, out):
    _, block = place()
    for t in range(NT):
        chunk = jnp.where(block < HALF, t, NT - 1 - t)
        start = pl.multiple_of(chunk * CHUNK, CHUNK)
        for v in range(NV):
            out[v, pl.ds(start, CHUNK)] = shares[t, v * CHUNK : (v + 1) * CHUNK]


def f32(*shape):
    return jax.ShapeDtypeStruct(shape, jnp.float32)


def shards(state, far_field, face_index, face_weight, mean_flow):
    matrix = jnp.asarray(level_matrix())
    t = lax.axis_index("tm")
    shares = pl.pallas_call(
        pack_kernel, out_shape=f32(NT, NR, W), in_specs=[VMEM] * 4, out_specs=VMEM, compiler_params=params(16), name="pack"
    )(state[0], far_field[0], face_index, face_weight[0])
    lines = lax.all_to_all(shares, "tm", 0, 0, tiled=True).reshape(NT * NR, W)
    low, high, left, right = pl.pallas_call(
        zone_kernel,
        out_shape=[f32(HALF_ZONE * NT, W)] * 2 + [f32(EDGE_PACKS * NT, W)] * 2,
        in_specs=[VMEM],
        out_specs=[VMEM] * 4,
        compiler_params=params(16),
        name="zone",
    )(lines)
    last = NT - 1
    given = lax.ppermute(low, "tm", [(last, last - 1)])
    offered = jnp.where(t == last - 1, given, high)
    rights = [(b, b // HALF * HALF + (b + 1) % HALF) for b in range(BLOCKS)]
    from_left = lax.ppermute(right, "block", rights)
    from_right = lax.ppermute(left, "block", [(b, a) for a, b in rights])
    zone_high = lax.all_to_all(jnp.broadcast_to(offered, (BLOCKS, HALF_ZONE * NT, W)), "block", 0, 0, tiled=True)
    zone_low = lax.ppermute(zone_high, "tm", [(last - 1, last)])
    ghosts = pl.pallas_call(
        chain_kernel,
        out_shape=f32(5, NV, 2, NT, W),
        in_specs=[VMEM] * 3 + [SMEM],
        out_specs=VMEM,
        scratch_shapes=[pltpu.VMEM((2, 2, 4, NV, HALF, NT, W), jnp.float32), pltpu.VMEM((2, NV, HALF, NT, W), jnp.float32)],
        compiler_params=params(32),
        name="chain",
    )(zone_low, zone_high, matrix, mean_flow)
    grid = pltpu.VMEM((LINES, NV * NT, 2 * W), jnp.float32)
    done = pl.pallas_call(
        bulk_kernel,
        out_shape=f32(NT * NV * CHUNK, W),
        in_specs=[VMEM] * 5 + [SMEM],
        out_specs=VMEM,
        scratch_shapes=[grid, grid, grid],
        compiler_params=params(32),
        name="bulk",
    )(lines, from_left, from_right, ghosts, matrix, mean_flow)
    done = lax.all_to_all(done.reshape(NT, NV * CHUNK, W), "tm", 0, 0, tiled=True)
    result = pl.pallas_call(
        unpack_kernel, out_shape=f32(NV, NT * CHUNK, W), in_specs=[VMEM], out_specs=VMEM, compiler_params=params(16), name="unpack"
    )(done)
    return result[None]


def solution(mesh):
    in_specs = (
        P("tm", None, None, "block"),
        P("tm", None, "block"),
        P("tm", "block"),
        P("tm", None, "block"),
        P(),
    )
    out_specs = P("tm", None, None, "block")
    return jax.shard_map(shards, mesh=mesh, in_specs=in_specs, out_specs=out_specs, check_vma=False)
```

```python
import jax
import jax.numpy as jnp
import ml_dtypes
import numpy as np
from jax import lax
from jax.experimental import pallas as pl
from jax.experimental.pallas import tpu as pltpu
from jax.sharding import PartitionSpec as P

SECTION_FACTORS = (0.075, 0.05, 0.1125, 0.15, 0.3)
OMEGA = 1.0
DISSIPATION = 0.2

NT = 16
NV = 4
CHUNK = 16
HALO = 5
LINES = CHUNK + 2 * HALO
W = 128
HALF = 8
BLOCKS = 16
NR = 112
BEFORE, AFTER, TABLE = 64, 84, 104
ZONE = 25
HALF_ZONE = 13
EDGE_PACKS = 7
VMEM = pl.BlockSpec(memory_space=pltpu.VMEM)
SMEM = pl.BlockSpec(memory_space=pltpu.SMEM)


def level_matrix():
    offsets = np.arange(NT)[:, None] - np.arange(NT)[None, :]
    angle = np.pi * offsets / NT
    safe = np.where(offsets == 0, 0.5 * np.pi, angle)
    cot = np.cos(safe) / np.sin(safe)
    matrix = np.where(offsets == 0, 0.0, 0.5 * (1.0 - 2.0 * (offsets % 2)) * cot)
    matrix = OMEGA * matrix + 4.0 * DISSIPATION * np.eye(NT)
    matrix = np.kron(np.eye(NV), matrix).astype(np.float32)
    lead = matrix.astype(ml_dtypes.bfloat16)
    rest = (matrix - lead.astype(np.float32)).astype(ml_dtypes.bfloat16)
    return np.concatenate([lead, rest, lead], axis=1)


def params(mib):
    return pltpu.CompilerParams(vmem_limit_bytes=mib << 20)


def place():
    return lax.axis_index("tm"), lax.axis_index("block")


def line_address(side, r, v):
    if r < 0:
        rotor, stator = BEFORE + v * HALO + r + HALO, AFTER + v * HALO - 1 - r
    elif r < CHUNK:
        rotor, stator = v * CHUNK + r, v * CHUNK + CHUNK - 1 - r
    else:
        rotor, stator = AFTER + v * HALO + r - CHUNK, BEFORE + v * HALO + 20 - r
    return jnp.where(side == 0, rotor, stator)


def pack_kernel(state, far, index, weight, out):
    _, block = place()
    side = block // HALF
    rotor = side == 0
    table = jnp.concatenate([index[...].astype(jnp.float32), weight[...], jnp.zeros((3, W), jnp.float32)], axis=0)
    for t in range(NT):
        chunk = jnp.where(rotor, t, NT - 1 - t)
        start = pl.multiple_of(chunk * CHUNK, CHUNK)
        low = pl.multiple_of(jnp.maximum(start - 8, 0), 8)
        high = pl.multiple_of(jnp.minimum(start + CHUNK, 248), 8)
        for v in range(NV):
            out[t, v * CHUNK : (v + 1) * CHUNK] = state[v, pl.ds(start, CHUNK)]
            before = state[v, pl.ds(low, 8)][3:8]
            after = state[v, pl.ds(high, 8)][0:5]
            if t == 0:
                ghost = jnp.broadcast_to(far[v : v + 1], (HALO, W))
                before = jnp.where(rotor, ghost, before)
                after = jnp.where(rotor, after, ghost)
            out[t, BEFORE + v * HALO : BEFORE + (v + 1) * HALO] = before
            out[t, AFTER + v * HALO : AFTER + (v + 1) * HALO] = after
        out[t, TABLE:NR] = table


def zone_kernel(lines, low, high, left, right):
    _, block = place()
    side = block // HALF
    for k in range(ZONE):
        if k < 20:
            address = line_address(side, CHUNK - 1 - k // NV, k % NV)
        else:
            address = TABLE + k - 20
        tile = lines[pl.ds(address, NT, stride=NR), :]
        if k < HALF_ZONE:
            low[k * NT : (k + 1) * NT] = tile
        else:
            high[(k - HALF_ZONE) * NT : (k - HALF_ZONE + 1) * NT] = tile
    high[(HALF_ZONE - 1) * NT :] = jnp.zeros((NT, W), jnp.float32)
    part = lax.broadcasted_iota(jnp.int32, (NT, W), 1) // 8
    for p in range(EDGE_PACKS):
        left_pack = jnp.zeros((NT, W), jnp.float32)
        right_pack = jnp.zeros((NT, W), jnp.float32)
        for k in range(16):
            m = p * 16 + k
            if m >= LINES * NV:
                break
            tile = lines[pl.ds(line_address(side, m // NV - HALO, m % NV), NT, stride=NR), :]
            moved = tile if k == 0 else pltpu.roll(tile, 8 * k, 1)
            left_pack = jnp.where(part == k, moved, left_pack)
            moved = tile if k == 15 else pltpu.roll(tile, 8 * k + 8, 1)
            right_pack = jnp.where(part == k, moved, right_pack)
        left[p * NT : (p + 1) * NT] = left_pack
        right[p * NT : (p + 1) * NT] = right_pack


def coefficients(flow, side):
    sign = jnp.where(side == 0, 0.5, -0.5)
    along = sign * flow[side, 0]
    across = 0.5 * flow[side, 1]
    return sign, along - DISSIPATION, -along - DISSIPATION, across - DISSIPATION, -across - DISSIPATION


def rates(coefs, up, down, nxt, prv, timed):
    sign, cu, cd, cn, cp = coefs
    plain = [timed[v] + (cu * up[v] + cd * down[v]) + (cn * nxt[v] + cp * prv[v]) for v in range(NV)]
    mixed = sign * (up[1] - down[1]) + 0.5 * (nxt[2] - prv[2])
    pressure_up = sign * (up[3] - down[3])
    pressure_next = 0.5 * (nxt[3] - prv[3])
    return [plain[0] + mixed, plain[1] + pressure_up, plain[2] + pressure_next, plain[3] + mixed]


def level_product(matrix, values):
    lead = values.astype(jnp.bfloat16)
    rest = (values - lead.astype(jnp.float32)).astype(jnp.bfloat16)
    return jnp.dot(matrix, jnp.concatenate([lead, lead, rest], axis=0), preferred_element_type=jnp.float32)


def split(lines):
    return [lines[v * NT : (v + 1) * NT] for v in range(NV)]


def chain_kernel(low, high, matrix, flow, out, cur, nexts, prevs, ghosts):
    _, block = place()
    own_side, own = block // HALF, block % HALF
    lane = lax.broadcasted_iota(jnp.int32, (NT, W), 1)

    def tile(side, j, k):
        source, k = (low, k) if k < HALF_ZONE else (high, k - HALF_ZONE)
        return source[HALF * side + j, k * NT : (k + 1) * NT, :]

    def value(section, side, line, v, j):
        if section == 0:
            return tile(side, j, line * NV + v)
        return cur[section % 2, side, line, v, j]

    def keep_rolled(section, side, line, v, j, values):
        nexts[section % 2, side, line, v, j] = pltpu.roll(values, W - 1, 1)
        prevs[section % 2, side, line, v, j] = pltpu.roll(values, 1, 1)

    def interpolate(section, side, j):
        first = tile(side, j, 20).astype(jnp.int32)
        parts = []
        for h in range(2):
            at = slice(8 * h, 8 * h + 8)
            totals = [None] * NV
            for k in range(4):
                source = (first[at] + k) & (HALF * W - 1)
                within, which = source & (W - 1), source >> 7
                weight = tile(side, j, 21 + k)[at]
                picked = [None] * NV
                for m in range(HALF):
                    here = which == m
                    for v in range(NV):
                        face = value(section, 1 - side, 0, v, m)[at]
                        got = jnp.take_along_axis(face, within, axis=1, mode="promise_in_bounds")
                        picked[v] = got if m == 0 else jnp.where(here, got, picked[v])
                totals = [weight * picked[v] if k == 0 else totals[v] + weight * picked[v] for v in range(NV)]
            parts.append(totals)
        return [jnp.concatenate([parts[0][v], parts[1][v]], axis=0) for v in range(NV)]

    def first_rolls(step, _):
        side, j = step // HALF, step % HALF
        for line in range(4):
            for v in range(NV):
                keep_rolled(0, side, line, v, j, value(0, side, line, v, j))
        return 0

    lax.fori_loop(0, 2 * HALF, first_rolls, 0)
    for s in range(4):

        def section_step(step, _, s=s):
            side, j = step // HALF, step % HALF
            after, before = (j + 1) % HALF, (j + HALF - 1) % HALF
            coefs = coefficients(flow, side)
            ghost = interpolate(s, side, j)
            for v in range(NV):
                ghosts[side, v, j] = ghost[v]
            lines = 4 - s
            here = [[value(s, side, line, v, j) for v in range(NV)] for line in range(lines + 1)]
            product = level_product(
                matrix[...], jnp.concatenate([jnp.concatenate(here[line], axis=0) for line in range(lines)], axis=1)
            )
            for line in reversed(range(lines)):
                up = ghost if line == 0 else here[line - 1]
                nxt = [
                    jnp.where(lane == W - 1, nexts[s % 2, side, line, v, after], nexts[s % 2, side, line, v, j])
                    for v in range(NV)
                ]
                prv = [
                    jnp.where(lane == 0, prevs[s % 2, side, line, v, before], prevs[s % 2, side, line, v, j])
                    for v in range(NV)
                ]
                timed = split(product[:, line * W : (line + 1) * W])
                rate = rates(coefs, up, here[line + 1], nxt, prv, timed)
                for v in range(NV):
                    result = value(0, side, line, v, j) - SECTION_FACTORS[s] * rate[v]
                    cur[(s + 1) % 2, side, line, v, j] = result
                    if line < lines - 1:
                        keep_rolled(s + 1, side, line, v, j, result)
            return 0

        lax.fori_loop(0, 2 * HALF, section_step, 0)
        for v in range(NV):
            out[s, v, 0] = ghosts[own_side, v, own]
            after = ghosts[own_side, v, (own + 1) % HALF]
            before = ghosts[own_side, v, (own + HALF - 1) % HALF]
            out[s, v, 1] = jnp.where(lane < W // 2, after, before)
    got = interpolate(4, own_side, own)
    for v in range(NV):
        out[4, v, 0] = got[v]
        out[4, v, 1] = got[v]


def bulk_kernel(lines, from_left, from_right, ghosts, matrix, flow, out, start, even, odd):
    t, block = place()
    side = block // HALF
    lane = lax.broadcasted_iota(jnp.int32, (NT, W), 1)
    for m in range(LINES * NV):
        r, v = m // NV - HALO, m % NV
        at = slice(v * NT, (v + 1) * NT)
        start[m // NV, at, :W] = lines[pl.ds(line_address(side, r, v), NT, stride=NR), :]
        p, k = m // 16, m % 16
        after = from_right[p * NT : (p + 1) * NT]
        after = after if k == 0 else pltpu.roll(after, W - 8 * k, 1)
        before = from_left[p * NT : (p + 1) * NT]
        before = before if k == 15 else pltpu.roll(before, 120 - 8 * k, 1)
        start[m // NV, at, W:] = jnp.where(lane < W // 2, after, before)
    coefs = coefficients(flow, side)
    group = 4
    for s in range(5):
        now = start if s == 0 else (even if s % 2 == 0 else odd)
        new = odd if s % 2 == 0 else even

        @pl.when(t == NT - 1)
        def _(now=now, s=s):
            for v in range(NV):
                at = slice(v * NT, (v + 1) * NT)
                now[HALO + CHUNK, at, :W] = ghosts[s, v, 0]
                now[HALO + CHUNK, at, W:] = ghosts[s, v, 1]

        if s > 0:

            @pl.when(t == 0)
            def _(now=now):
                now[HALO - 1] = start[HALO - 1]

        first = (1, 1, 3, 3, 5)[s]

        def line_step(step, _, now=now, new=new, s=s, first=first):
            i = first + group * step
            here = [now[i - 1 + g] for g in range(group + 2)]
            product = level_product(matrix[...], jnp.concatenate(here[1:-1], axis=1))
            for g in range(group):
                line = here[g + 1]
                nxt = pltpu.roll(line, 2 * W - 1, 1)
                prv = pltpu.roll(line, 1, 1)
                timed = split(product[:, 2 * W * g : 2 * W * (g + 1)])
                rate = rates(coefs, split(here[g + 2]), split(here[g]), split(nxt), split(prv), timed)
                base = split(start[i + g])
                for v in range(NV):
                    result = base[v] - SECTION_FACTORS[s] * rate[v]
                    if s < 4:
                        new[i + g, v * NT : (v + 1) * NT] = result
                    else:
                        cell = jnp.where(side == 0, i + g - HALO, CHUNK - 1 + HALO - i - g)
                        out[pl.ds(v * CHUNK + cell, NT, stride=NV * CHUNK), :] = result[:, :W]
            return 0

        lax.fori_loop(0, (LINES - 2 * first) // group, line_step, 0)


def unpack_kernel(shares, out):
    _, block = place()
    for t in range(NT):
        chunk = jnp.where(block < HALF, t, NT - 1 - t)
        start = pl.multiple_of(chunk * CHUNK, CHUNK)
        for v in range(NV):
            out[v, pl.ds(start, CHUNK)] = shares[t, v * CHUNK : (v + 1) * CHUNK]


def f32(*shape):
    return jax.ShapeDtypeStruct(shape, jnp.float32)


def shards(state, far_field, face_index, face_weight, mean_flow):
    matrix = jnp.asarray(level_matrix())
    t = lax.axis_index("tm")
    shares = pl.pallas_call(
        pack_kernel, out_shape=f32(NT, NR, W), in_specs=[VMEM] * 4, out_specs=VMEM, compiler_params=params(16), name="pack"
    )(state[0], far_field[0], face_index, face_weight[0])
    lines = lax.all_to_all(shares, "tm", 0, 0, tiled=True).reshape(NT * NR, W)
    low, high, left, right = pl.pallas_call(
        zone_kernel,
        out_shape=[f32(HALF_ZONE * NT, W)] * 2 + [f32(EDGE_PACKS * NT, W)] * 2,
        in_specs=[VMEM],
        out_specs=[VMEM] * 4,
        compiler_params=params(16),
        name="zone",
    )(lines)
    last = NT - 1
    given = lax.ppermute(low, "tm", [(last, last - 1)])
    offered = jnp.where(t == last - 1, given, high)
    rights = [(b, b // HALF * HALF + (b + 1) % HALF) for b in range(BLOCKS)]
    from_left = lax.ppermute(right, "block", rights)
    from_right = lax.ppermute(left, "block", [(b, a) for a, b in rights])
    zone_high = lax.all_to_all(jnp.broadcast_to(offered, (BLOCKS, HALF_ZONE * NT, W)), "block", 0, 0, tiled=True)
    zone_low = lax.ppermute(zone_high, "tm", [(last - 1, last)])
    ghosts = pl.pallas_call(
        chain_kernel,
        out_shape=f32(5, NV, 2, NT, W),
        in_specs=[VMEM] * 3 + [SMEM],
        out_specs=VMEM,
        scratch_shapes=[pltpu.VMEM((2, 2, 4, NV, HALF, NT, W), jnp.float32)] * 3
        + [pltpu.VMEM((2, NV, HALF, NT, W), jnp.float32)],
        compiler_params=params(32),
        name="chain",
    )(zone_low, zone_high, matrix, mean_flow)
    grid = pltpu.VMEM((LINES, NV * NT, 2 * W), jnp.float32)
    done = pl.pallas_call(
        bulk_kernel,
        out_shape=f32(NT * NV * CHUNK, W),
        in_specs=[VMEM] * 5 + [SMEM],
        out_specs=VMEM,
        scratch_shapes=[grid, grid, grid],
        compiler_params=params(32),
        name="bulk",
    )(lines, from_left, from_right, ghosts, matrix, mean_flow)
    done = lax.all_to_all(done.reshape(NT, NV * CHUNK, W), "tm", 0, 0, tiled=True)
    result = pl.pallas_call(
        unpack_kernel, out_shape=f32(NV, NT * CHUNK, W), in_specs=[VMEM], out_specs=VMEM, compiler_params=params(16), name="unpack"
    )(done)
    return result[None]


def solution(mesh):
    in_specs = (
        P("tm", None, None, "block"),
        P("tm", None, "block"),
        P("tm", "block"),
        P("tm", None, "block"),
        P(),
    )
    out_specs = P("tm", None, None, "block")
    return jax.shard_map(shards, mesh=mesh, in_specs=in_specs, out_specs=out_specs, check_vma=False)
```

```python
import jax
import jax.numpy as jnp
import ml_dtypes
import numpy as np
from jax import lax
from jax.experimental import pallas as pl
from jax.experimental.pallas import tpu as pltpu
from jax.sharding import PartitionSpec as P

SECTION_FACTORS = (0.075, 0.05, 0.1125, 0.15, 0.3)
OMEGA = 1.0
DISSIPATION = 0.2

NT = 16
NV = 4
CHUNK = 16
HALO = 5
LINES = CHUNK + 2 * HALO
W = 128
HALF = 8
BLOCKS = 16
NR = 112
BEFORE, AFTER, TABLE = 64, 84, 104
ZONE = 25
HALF_ZONE = 13
EDGE_PACKS = 7
VMEM = pl.BlockSpec(memory_space=pltpu.VMEM)
SMEM = pl.BlockSpec(memory_space=pltpu.SMEM)


def level_matrix():
    offsets = np.arange(NT)[:, None] - np.arange(NT)[None, :]
    angle = np.pi * offsets / NT
    safe = np.where(offsets == 0, 0.5 * np.pi, angle)
    cot = np.cos(safe) / np.sin(safe)
    matrix = np.where(offsets == 0, 0.0, 0.5 * (1.0 - 2.0 * (offsets % 2)) * cot)
    matrix = OMEGA * matrix + 4.0 * DISSIPATION * np.eye(NT)
    matrix = np.kron(np.eye(NV), matrix).astype(np.float32)
    lead = matrix.astype(ml_dtypes.bfloat16)
    rest = (matrix - lead.astype(np.float32)).astype(ml_dtypes.bfloat16)
    return np.concatenate([lead, rest, lead], axis=1)


def params(mib):
    return pltpu.CompilerParams(vmem_limit_bytes=mib << 20)


def place():
    return lax.axis_index("tm"), lax.axis_index("block")


def line_address(side, r, v):
    if r < 0:
        rotor, stator = BEFORE + v * HALO + r + HALO, AFTER + v * HALO - 1 - r
    elif r < CHUNK:
        rotor, stator = v * CHUNK + r, v * CHUNK + CHUNK - 1 - r
    else:
        rotor, stator = AFTER + v * HALO + r - CHUNK, BEFORE + v * HALO + 20 - r
    return jnp.where(side == 0, rotor, stator)


def pack_kernel(state_in, far_in, index_in, weight_in, out, state, far, index, weight, sems):
    copies = [
        pltpu.make_async_copy(source, target, sems.at[i])
        for i, (source, target) in enumerate(
            ((state_in, state), (far_in, far), (index_in, index), (weight_in, weight))
        )
    ]
    for copy in copies:
        copy.start()
    _, block = place()
    side = block // HALF
    rotor = side == 0
    for copy in copies:
        copy.wait()
    table = jnp.concatenate([index[...].astype(jnp.float32), weight[...], jnp.zeros((3, W), jnp.float32)], axis=0)
    for t in range(NT):
        chunk = jnp.where(rotor, t, NT - 1 - t)
        start = pl.multiple_of(chunk * CHUNK, CHUNK)
        low = pl.multiple_of(jnp.maximum(start - 8, 0), 8)
        high = pl.multiple_of(jnp.minimum(start + CHUNK, 248), 8)
        for v in range(NV):
            out[t, v * CHUNK : (v + 1) * CHUNK] = state[v, pl.ds(start, CHUNK)]
            before = state[v, pl.ds(low, 8)][3:8]
            after = state[v, pl.ds(high, 8)][0:5]
            if t == 0:
                ghost = jnp.broadcast_to(far[v : v + 1], (HALO, W))
                before = jnp.where(rotor, ghost, before)
                after = jnp.where(rotor, after, ghost)
            out[t, BEFORE + v * HALO : BEFORE + (v + 1) * HALO] = before
            out[t, AFTER + v * HALO : AFTER + (v + 1) * HALO] = after
        out[t, TABLE:NR] = table


def zone_kernel(lines, low, high, left, right):
    _, block = place()
    side = block // HALF
    for k in range(ZONE):
        if k < 20:
            address = line_address(side, CHUNK - 1 - k // NV, k % NV)
        else:
            address = TABLE + k - 20
        tile = lines[pl.ds(address, NT, stride=NR), :]
        if k < HALF_ZONE:
            low[k * NT : (k + 1) * NT] = tile
        else:
            high[(k - HALF_ZONE) * NT : (k - HALF_ZONE + 1) * NT] = tile
    high[(HALF_ZONE - 1) * NT :] = jnp.zeros((NT, W), jnp.float32)
    part = lax.broadcasted_iota(jnp.int32, (NT, W), 1) // 8
    for p in range(EDGE_PACKS):
        left_pack = jnp.zeros((NT, W), jnp.float32)
        right_pack = jnp.zeros((NT, W), jnp.float32)
        for k in range(16):
            m = p * 16 + k
            if m >= LINES * NV:
                break
            tile = lines[pl.ds(line_address(side, m // NV - HALO, m % NV), NT, stride=NR), :]
            moved = tile if k == 0 else pltpu.roll(tile, 8 * k, 1)
            left_pack = jnp.where(part == k, moved, left_pack)
            moved = tile if k == 15 else pltpu.roll(tile, 8 * k + 8, 1)
            right_pack = jnp.where(part == k, moved, right_pack)
        left[p * NT : (p + 1) * NT] = left_pack
        right[p * NT : (p + 1) * NT] = right_pack


def coefficients(flow, side):
    sign = jnp.where(side == 0, 0.5, -0.5)
    along = sign * flow[side, 0]
    across = 0.5 * flow[side, 1]
    return sign, along - DISSIPATION, -along - DISSIPATION, across - DISSIPATION, -across - DISSIPATION


def rates(coefs, up, down, nxt, prv, timed):
    sign, cu, cd, cn, cp = coefs
    plain = [timed[v] + (cu * up[v] + cd * down[v]) + (cn * nxt[v] + cp * prv[v]) for v in range(NV)]
    mixed = sign * (up[1] - down[1]) + 0.5 * (nxt[2] - prv[2])
    pressure_up = sign * (up[3] - down[3])
    pressure_next = 0.5 * (nxt[3] - prv[3])
    return [plain[0] + mixed, plain[1] + pressure_up, plain[2] + pressure_next, plain[3] + mixed]


def level_product(matrix, values):
    lead = values.astype(jnp.bfloat16)
    rest = (values - lead.astype(jnp.float32)).astype(jnp.bfloat16)
    return jnp.dot(matrix, jnp.concatenate([lead, lead, rest], axis=0), preferred_element_type=jnp.float32)


def split(lines):
    return [lines[v * NT : (v + 1) * NT] for v in range(NV)]


def chain_kernel(low, high, table, matrix, flow, done, out, cur, nexts, prevs, shifted, ordered, weighed, ghosts, applied):
    t, block = place()
    own_side, own = block // HALF, block % HALF
    lane = lax.broadcasted_iota(jnp.int32, (NT, W), 1)
    out[...] = done[...]

    def tile(side, j, k):
        source, k = (low, k) if k < HALF_ZONE else (high, k - HALF_ZONE)
        return source[HALF * side + j, k * NT : (k + 1) * NT, :]

    def value(section, side, line, v, j):
        if section == 0:
            return tile(side, j, line * NV + v)
        return cur[section % 2, side, line, v, j]

    def keep_rolled(section, side, line, v, j, values, shift=False):
        nexts[section % 2, side, line, v, j] = pltpu.roll(values, W - 1, 1)
        prevs[section % 2, side, line, v, j] = pltpu.roll(values, 1, 1)
        if shift:
            shifted[0, side, v, j] = pltpu.roll(values, W - 2, 1)
            shifted[1, side, v, j] = pltpu.roll(values, W - 3, 1)

    def interpolate_first(side, j):
        first = tile(side, j, 20).astype(jnp.int32)
        parts = []
        for h in range(2):
            at = slice(8 * h, 8 * h + 8)
            totals = [None] * NV
            for k in range(4):
                source = (first[at] + k) & (HALF * W - 1)
                within, which = source & (W - 1), source >> 7
                weight = tile(side, j, 21 + k)[at]
                picked = [None] * NV
                for m in range(HALF):
                    here = which == m
                    for v in range(NV):
                        face = value(0, 1 - side, 0, v, m)[at]
                        got = jnp.take_along_axis(face, within, axis=1, mode="promise_in_bounds")
                        picked[v] = got if m == 0 else jnp.where(here, got, picked[v])
                totals = [weight * picked[v] if k == 0 else totals[v] + weight * picked[v] for v in range(NV)]
            parts.append(totals)
        return [jnp.concatenate([parts[0][v], parts[1][v]], axis=0) for v in range(NV)]

    def order_weights(side, level):
        rows = lambda k: table[pl.ds(HALF * side * HALF_ZONE * NT + (7 + k) * NT + level, HALF, stride=HALF_ZONE * NT), :]
        first = rows(0).astype(jnp.int32)
        within, which = first & (W - 1), first >> 7
        weight = [rows(1 + k) for k in range(4)]
        eight = lax.broadcasted_iota(jnp.int32, (HALF, W), 0)
        many = lax.broadcasted_iota(jnp.int32, (W, W), 0)
        spread, chosen = [], []
        for j in range(HALF):
            here = jnp.broadcast_to(which[j : j + 1], (HALF, W)) == eight
            spread.append(
                jnp.concatenate(
                    [jnp.where(here, jnp.broadcast_to(weight[k][j : j + 1], (HALF, W)), 0.0) for k in range(4)], axis=0
                )
            )
            hit = jnp.broadcast_to(within[j : j + 1], (W, W)) == many
            chosen.append(jnp.where(hit, 1.0, 0.0).astype(jnp.bfloat16))
        spread = jnp.concatenate(spread, axis=1)
        chosen = jnp.concatenate(chosen, axis=1)
        lead = spread.astype(jnp.bfloat16)
        rest = (spread - lead.astype(jnp.float32)).astype(jnp.bfloat16)
        both = lax.dot_general(
            jnp.concatenate([lead, rest], axis=0), chosen, (((1,), (1,)), ((), ())), preferred_element_type=jnp.float32
        )
        both = both[:32] + both[32:]
        for k in range(4):
            ordered[side, k, pl.ds(level, HALF, stride=NT), :] = both[8 * k : 8 * k + 8]

    def weigh(section, side, m):
        other, after = 1 - side, (m + 1) % HALF
        weight = [ordered[side, k, pl.ds(pl.multiple_of(m * NT, NT), NT), :] for k in range(4)]
        for v in range(NV):
            total = weight[0] * value(section, other, 0, v, m)
            for k in range(1, 4):
                if k == 1:
                    here, there = nexts[section % 2, other, 0, v, m], nexts[section % 2, other, 0, v, after]
                else:
                    here, there = shifted[k - 2, other, v, m], shifted[k - 2, other, v, after]
                total = total + weight[k] * jnp.where(lane >= W - k, there, here)
            weighed[side, v, m] = total

    def interpolate(side, j):
        first = tile(side, j, 20).astype(jnp.int32)
        within, which = first & (W - 1), first >> 7
        parts = []
        for h in range(2):
            at = slice(8 * h, 8 * h + 8)
            picked = [None] * NV
            for m in range(HALF):
                here = which[at] == m
                for v in range(NV):
                    got = jnp.take_along_axis(weighed[side, v, m, at], within[at], axis=1, mode="promise_in_bounds")
                    picked[v] = got if m == 0 else jnp.where(here, got, picked[v])
            parts.append(picked)
        return [jnp.concatenate([parts[0][v], parts[1][v]], axis=0) for v in range(NV)]

    def first_rolls(step, _):
        side, j = step // HALF, step % HALF
        for line in range(4):
            for v in range(NV):
                keep_rolled(0, side, line, v, j, value(0, side, line, v, j))
        return 0

    lax.fori_loop(0, 2 * HALF, first_rolls, 0)
    for s in range(4):
        first_side, steps = (0, 2 * HALF) if s < 3 else (1 - own_side, HALF)

        def weigh_step(step, _, s=s):
            weigh(s, step // HALF, step % HALF)
            return 0

        def section_step(step, _, s=s, first_side=first_side):
            side, j = first_side + step // HALF, step % HALF
            after, before = (j + 1) % HALF, (j + HALF - 1) % HALF
            coefs = coefficients(flow, side)
            ghost = interpolate_first(side, j) if s == 0 else interpolate(side, j)
            for v in range(NV):
                ghosts[s % 2, side, v, j] = ghost[v]
            lines = 4 - s
            here = [[value(s, side, line, v, j) for v in range(NV)] for line in range(lines + 1)]
            product = level_product(
                matrix[...], jnp.concatenate([jnp.concatenate(here[line], axis=0) for line in range(lines)], axis=1)
            )
            for line in reversed(range(lines)):
                up = ghost if line == 0 else here[line - 1]
                nxt = [
                    jnp.where(lane == W - 1, nexts[s % 2, side, line, v, after], nexts[s % 2, side, line, v, j])
                    for v in range(NV)
                ]
                prv = [
                    jnp.where(lane == 0, prevs[s % 2, side, line, v, before], prevs[s % 2, side, line, v, j])
                    for v in range(NV)
                ]
                timed = split(product[:, line * W : (line + 1) * W])
                rate = rates(coefs, up, here[line + 1], nxt, prv, timed)
                for v in range(NV):
                    result = value(0, side, line, v, j) - SECTION_FACTORS[s] * rate[v]
                    cur[(s + 1) % 2, side, line, v, j] = result
                    if line < max(lines - 1, 1):
                        keep_rolled(s + 1, side, line, v, j, result, line == 0)
            if s == 0:
                order_weights(side, 2 * j)
                order_weights(side, 2 * j + 1)
            return 0

        if s > 0:
            lax.fori_loop(0, 2 * HALF, weigh_step, 0)
        lax.fori_loop(0, steps, section_step, 0)
        if s == 3:

            def own_step(step, _):
                j = (own + HALF - 1 + step) % HALF
                ghost = interpolate(own_side, j)
                for v in range(NV):
                    ghosts[1, own_side, v, j] = ghost[v]
                return 0

            lax.fori_loop(0, 3, own_step, 0)
        for v in range(NV):
            at = slice(v * NT, (v + 1) * NT)
            applied[s, at, :W] = ghosts[s % 2, own_side, v, own]
            after = ghosts[s % 2, own_side, v, (own + 1) % HALF]
            before = ghosts[s % 2, own_side, v, (own + HALF - 1) % HALF]
            applied[s, at, W:] = jnp.where(lane < W // 2, after, before)

    def last_weigh(m, _):
        weigh(4, own_side, m)
        return 0

    lax.fori_loop(0, HALF, last_weigh, 0)
    got = interpolate(own_side, own)
    for v in range(NV):
        at = slice(v * NT, (v + 1) * NT)
        applied[4, at, :W] = got[v]
        applied[4, at, W:] = got[v]

    coefs = coefficients(flow, own_side)
    zero = jnp.zeros((NV * NT, 2 * W), jnp.float32)
    response = []
    for s in range(5):
        product = None
        if s:
            product = level_product(matrix[...], jnp.concatenate(response, axis=1))
        padded = [applied[s]] + response + [zero, zero]
        new = []
        for line in range(s + 1):
            here = padded[line + 1]
            if line < s:
                nxt, prv = pltpu.roll(here, 2 * W - 1, 1), pltpu.roll(here, 1, 1)
                timed = product[:, 2 * W * line : 2 * W * (line + 1)]
            else:
                nxt = prv = timed = zero
            rate = rates(coefs, split(padded[line]), split(padded[line + 2]), split(nxt), split(prv), split(timed))
            new.append(-SECTION_FACTORS[s] * jnp.concatenate(rate, axis=0))
        response = new

    @pl.when(t == NT - 1)
    def _():
        for line in range(HALO):
            for v in range(NV):
                cell = jnp.where(own_side == 0, CHUNK - 1 - line, line)
                at = pl.ds(v * CHUNK + cell, NT, stride=NV * CHUNK)
                out[at, :] = done[at, :] + response[line][v * NT : (v + 1) * NT, :W]


def bulk_kernel(lines, from_left, from_right, matrix, flow, out, start, even, odd):
    t, block = place()
    side = block // HALF
    lane = lax.broadcasted_iota(jnp.int32, (NT, W), 1)
    for m in range(LINES * NV):
        r, v = m // NV - HALO, m % NV
        at = slice(v * NT, (v + 1) * NT)
        start[m // NV, at, :W] = lines[pl.ds(line_address(side, r, v), NT, stride=NR), :]
        p, k = m // 16, m % 16
        after = from_right[p * NT : (p + 1) * NT]
        after = after if k == 0 else pltpu.roll(after, W - 8 * k, 1)
        before = from_left[p * NT : (p + 1) * NT]
        before = before if k == 15 else pltpu.roll(before, 120 - 8 * k, 1)
        start[m // NV, at, W:] = jnp.where(lane < W // 2, after, before)
    coefs = coefficients(flow, side)
    group = 4
    for s in range(5):
        now = start if s == 0 else (even if s % 2 == 0 else odd)
        new = odd if s % 2 == 0 else even

        @pl.when(t == NT - 1)
        def _(now=now):
            now[HALO + CHUNK] = jnp.zeros((NV * NT, 2 * W), jnp.float32)

        if s > 0:

            @pl.when(t == 0)
            def _(now=now):
                now[HALO - 1] = start[HALO - 1]

        first = (1, 1, 3, 3, 5)[s]

        def line_step(step, _, now=now, new=new, s=s, first=first):
            i = first + group * step
            here = [now[i - 1 + g] for g in range(group + 2)]
            product = level_product(matrix[...], jnp.concatenate(here[1:-1], axis=1))
            for g in range(group):
                line = here[g + 1]
                nxt = pltpu.roll(line, 2 * W - 1, 1)
                prv = pltpu.roll(line, 1, 1)
                timed = split(product[:, 2 * W * g : 2 * W * (g + 1)])
                rate = rates(coefs, split(here[g + 2]), split(here[g]), split(nxt), split(prv), timed)
                base = split(start[i + g])
                for v in range(NV):
                    result = base[v] - SECTION_FACTORS[s] * rate[v]
                    if s < 4:
                        new[i + g, v * NT : (v + 1) * NT] = result
                    else:
                        cell = jnp.where(side == 0, i + g - HALO, CHUNK - 1 + HALO - i - g)
                        out[pl.ds(v * CHUNK + cell, NT, stride=NV * CHUNK), :] = result[:, :W]
            return 0

        lax.fori_loop(0, (LINES - 2 * first) // group, line_step, 0)


def unpack_kernel(shares, out):
    _, block = place()
    for t in range(NT):
        chunk = jnp.where(block < HALF, t, NT - 1 - t)
        start = pl.multiple_of(chunk * CHUNK, CHUNK)
        for v in range(NV):
            out[v, pl.ds(start, CHUNK)] = shares[t, v * CHUNK : (v + 1) * CHUNK]


def f32(*shape):
    return jax.ShapeDtypeStruct(shape, jnp.float32)


def cost(flops, nbytes):
    return pl.CostEstimate(flops=flops, bytes_accessed=nbytes, transcendentals=0)


def shards(state, far_field, face_index, face_weight, mean_flow):
    matrix = jnp.asarray(level_matrix())
    t = lax.axis_index("tm")
    last = NT - 1
    shares = pl.pallas_call(
        pack_kernel,
        out_shape=f32(NT, NR, W),
        in_specs=[pl.BlockSpec(memory_space=pltpu.HBM)] * 4,
        out_specs=VMEM,
        scratch_shapes=[
            pltpu.VMEM((NV, NT * CHUNK, W), jnp.float32),
            pltpu.VMEM((NV, W), jnp.float32),
            pltpu.VMEM((1, W), jnp.int32),
            pltpu.VMEM((NV, W), jnp.float32),
            pltpu.SemaphoreType.DMA((4,)),
        ],
        compiler_params=params(16),
        name="pack",
    )(state[0], far_field[0], face_index, face_weight[0])
    lines = lax.all_to_all(shares, "tm", 0, 0, tiled=True).reshape(NT * NR, W)
    low, high, left, right = pl.pallas_call(
        zone_kernel,
        out_shape=[f32(HALF_ZONE * NT, W)] * 2 + [f32(EDGE_PACKS * NT, W)] * 2,
        in_specs=[VMEM],
        out_specs=[VMEM] * 4,
        compiler_params=params(16),
        name="zone",
    )(lines)
    rights = [(b, b // HALF * HALF + (b + 1) % HALF) for b in range(BLOCKS)]
    from_left = lax.ppermute(right, "block", rights)
    from_right = lax.ppermute(left, "block", [(b, a) for a, b in rights])
    given = lax.ppermute(low, "tm", [(last, last - 1)])
    given, from_left, from_right = lax.optimization_barrier((given, from_left, from_right))
    offered = jnp.where(t == last - 1, given, high)
    zone_high = lax.all_to_all(jnp.broadcast_to(offered, (BLOCKS, HALF_ZONE * NT, W)), "block", 0, 0, tiled=True)
    grid = pltpu.VMEM((LINES, NV * NT, 2 * W), jnp.float32)
    done = pl.pallas_call(
        bulk_kernel,
        out_shape=f32(NT * NV * CHUNK, W),
        in_specs=[VMEM] * 4 + [SMEM],
        out_specs=VMEM,
        scratch_shapes=[grid, grid, grid],
        compiler_params=params(24),
        cost_estimate=cost(2 * 10**9, 16 << 20),
        name="bulk",
    )(lines, from_left, from_right, matrix, mean_flow)
    zone_high, done = lax.optimization_barrier((zone_high, done))
    zone_low = lax.ppermute(zone_high, "tm", [(last - 1, last)])
    lines_of = pltpu.VMEM((2, 2, 4, NV, HALF, NT, W), jnp.float32)
    faces_of = pltpu.VMEM((2, 2, NV, HALF, NT, W), jnp.float32)
    done = pl.pallas_call(
        chain_kernel,
        out_shape=f32(NT * NV * CHUNK, W),
        in_specs=[VMEM] * 4 + [SMEM, VMEM],
        out_specs=VMEM,
        scratch_shapes=[lines_of] * 3
        + [faces_of]
        + [pltpu.VMEM((2, 4, HALF * NT, W), jnp.float32), pltpu.VMEM((2, NV, HALF, NT, W), jnp.float32)]
        + [faces_of, pltpu.VMEM((5, NV * NT, 2 * W), jnp.float32)],
        compiler_params=params(40),
        cost_estimate=cost(8 * 10**9, 64 << 20),
        name="chain",
    )(zone_low, zone_high, zone_high.reshape(BLOCKS * HALF_ZONE * NT, W), matrix, mean_flow, done)
    done = lax.all_to_all(done.reshape(NT, NV * CHUNK, W), "tm", 0, 0, tiled=True)
    result = pl.pallas_call(
        unpack_kernel,
        out_shape=f32(NV, NT * CHUNK, W),
        in_specs=[VMEM],
        out_specs=VMEM,
        compiler_params=params(16),
        name="unpack",
    )(done)
    return result[None]


def solution(mesh):
    in_specs = (
        P("tm", None, None, "block"),
        P("tm", None, "block"),
        P("tm", "block"),
        P("tm", None, "block"),
        P(),
    )
    out_specs = P("tm", None, None, "block")
    return jax.shard_map(shards, mesh=mesh, in_specs=in_specs, out_specs=out_specs, check_vma=False)
```

```python
import jax
import jax.numpy as jnp
import ml_dtypes
import numpy as np
from jax import lax
from jax.experimental import pallas as pl
from jax.experimental.pallas import tpu as pltpu
from jax.sharding import PartitionSpec as P

SECTION_FACTORS = (0.075, 0.05, 0.1125, 0.15, 0.3)
OMEGA = 1.0
DISSIPATION = 0.2

NT = 16
NV = 4
PARTS = 14
CHUNK = 19
HALO = 5
LINES = CHUNK + 2 * HALO
TAIL = 256 - (PARTS - 1) * CHUNK
W = 128
HALF = 8
BLOCKS = 16
NR = 80
ROW = 20
HALF_ZONE = 13
ENDS = HALO * NV
EDGE_PACKS = 8
FIRST_HALF = tuple(range(4, 17))
SECOND_HALF = (20, 21, 22, 23, 24, 0, 1, 2, 3, 17, 18, 19)
SU = (1, 2, 2, 4)
VMEM = pl.BlockSpec(memory_space=pltpu.VMEM)
SMEM = pl.BlockSpec(memory_space=pltpu.SMEM)


def level_matrix():
    offsets = np.arange(NT)[:, None] - np.arange(NT)[None, :]
    angle = np.pi * offsets / NT
    safe = np.where(offsets == 0, 0.5 * np.pi, angle)
    cot = np.cos(safe) / np.sin(safe)
    matrix = np.where(offsets == 0, 0.0, 0.5 * (1.0 - 2.0 * (offsets % 2)) * cot)
    matrix = OMEGA * matrix + 4.0 * DISSIPATION * np.eye(NT)
    matrix = np.kron(np.eye(NV), matrix).astype(np.float32)
    lead = matrix.astype(ml_dtypes.bfloat16)
    rest = (matrix - lead.astype(np.float32)).astype(ml_dtypes.bfloat16)
    return np.concatenate([lead, rest, lead], axis=1)


def params(mib):
    return pltpu.CompilerParams(vmem_limit_bytes=mib << 20)


def place():
    return lax.axis_index("tm"), lax.axis_index("block")


def pack_kernel(state_in, far_in, index_in, weight_in, out, state, far, index, weight, sems):
    copies = [
        pltpu.make_async_copy(source, target, sems.at[i])
        for i, (source, target) in enumerate(
            ((state_in, state), (far_in, far), (index_in, index), (weight_in, weight))
        )
    ]
    for copy in copies:
        copy.start()
    for copy in copies:
        copy.wait()
    _, block = place()

    def fill(rotor):
        for t in range(PARTS):
            first = t * CHUNK if rotor else 256 - (t + 1) * CHUNK
            skip = max(-first, 0)
            count = min(CHUNK, 256 - first) - skip
            for v in range(NV):
                at = v * ROW + skip
                out[t, at : at + count] = state[v, first + skip : first + skip + count]
                out[t, v * ROW + CHUNK : (v + 1) * ROW] = far[v : v + 1]
        lines = []
        for line in range(HALO):
            cell = 255 - line if rotor else line
            lines += [state[v, cell : cell + 1] for v in range(NV)]
        lines += [index[...].astype(jnp.float32)] + [weight[k : k + 1] for k in range(4)]
        for t, half in ((PARTS, FIRST_HALF), (PARTS + 1, SECOND_HALF)):
            for i, k in enumerate(half):
                out[t, i : i + 1] = lines[k]

    @pl.when(block < HALF)
    def _():
        fill(True)

    @pl.when(block >= HALF)
    def _():
        fill(False)


def line_address(side, r, v):
    return v * ROW + jnp.where(side == 0, r, CHUNK - 1 - r)


def zone_kernel(lines, zone, ends_up, ends_down):
    _, block = place()
    side = block // HALF
    for i in range(HALF_ZONE):
        tile = lines[pl.ds(i, NT, stride=NR), :]
        for b in range(BLOCKS):
            zone[b, i * NT : (i + 1) * NT] = tile
    for i in range(ENDS):
        r, v = i // NV, i % NV
        at = slice(i * NT, (i + 1) * NT)
        ends_up[at] = lines[pl.ds(line_address(side, CHUNK - HALO + r, v), NT, stride=NR), :]
        ends_down[at] = lines[pl.ds(line_address(side, r, v), NT, stride=NR), :]


def line_tile(lines, below, above, t, side, r, v):
    if r < 0:
        at = (r + HALO) * NV + v
        tile = below[at * NT : (at + 1) * NT]
        if r == -1:
            tile = jnp.where(t == 0, lines[pl.ds(v * ROW + CHUNK, NT, stride=NR), :], tile)
        return tile
    if r < CHUNK:
        return lines[pl.ds(line_address(side, r, v), NT, stride=NR), :]
    at = (r - CHUNK) * NV + v
    return above[at * NT : (at + 1) * NT]


def edge_kernel(lines, below, above, left, right):
    t, block = place()
    side = block // HALF
    part = lax.broadcasted_iota(jnp.int32, (NT, W), 1) // 8
    for p in range(EDGE_PACKS):
        left_pack = jnp.zeros((NT, W), jnp.float32)
        right_pack = jnp.zeros((NT, W), jnp.float32)
        for k in range(16):
            m = p * 16 + k
            if m >= LINES * NV:
                break
            tile = line_tile(lines, below, above, t, side, m // NV - HALO, m % NV)
            moved = tile if k == 0 else pltpu.roll(tile, 8 * k, 1)
            left_pack = jnp.where(part == k, moved, left_pack)
            moved = tile if k == 15 else pltpu.roll(tile, 8 * k + 8, 1)
            right_pack = jnp.where(part == k, moved, right_pack)
        left[p * NT : (p + 1) * NT] = left_pack
        right[p * NT : (p + 1) * NT] = right_pack


def coefficients(flow, side):
    sign = (0.5, -0.5)[side] if isinstance(side, int) else jnp.where(side == 0, 0.5, -0.5)
    along = sign * flow[side, 0]
    across = 0.5 * flow[side, 1]
    return sign, along - DISSIPATION, -along - DISSIPATION, across - DISSIPATION, -across - DISSIPATION


def rates(coefs, up, down, nxt, prv, timed):
    sign, cu, cd, cn, cp = coefs
    plain = [timed[v] + (cu * up[v] + cd * down[v]) + (cn * nxt[v] + cp * prv[v]) for v in range(NV)]
    mixed = sign * (up[1] - down[1]) + 0.5 * (nxt[2] - prv[2])
    pressure_up = sign * (up[3] - down[3])
    pressure_next = 0.5 * (nxt[3] - prv[3])
    return [plain[0] + mixed, plain[1] + pressure_up, plain[2] + pressure_next, plain[3] + mixed]


def level_product(matrix, values):
    lead = values.astype(jnp.bfloat16)
    rest = (values - lead.astype(jnp.float32)).astype(jnp.bfloat16)
    return jnp.dot(matrix, jnp.concatenate([lead, lead, rest], axis=0), preferred_element_type=jnp.float32)


def split(lines):
    return [lines[v * NT : (v + 1) * NT] for v in range(NV)]


def zone_tile(first_half, second_half, side, j, k):
    source, at = (first_half, FIRST_HALF.index(k)) if k in FIRST_HALF else (second_half, SECOND_HALF.index(k))
    return source[HALF * side + j, at * NT : (at + 1) * NT, :]


def start_kernel(high, table, ghosts, ordered):
    def tile(side, j, k):
        return zone_tile(None, high, side, j, k)

    def interpolate_first(side, j):
        first = tile(side, j, 20).astype(jnp.int32)
        parts = []
        for h in range(2):
            at = slice(8 * h, 8 * h + 8)
            totals = [None] * NV
            for k in range(4):
                source = (first[at] + k) & (HALF * W - 1)
                within, which = source & (W - 1), source >> 7
                weight = tile(side, j, 21 + k)[at]
                picked = [None] * NV
                for m in range(HALF):
                    here = which == m
                    for v in range(NV):
                        face = tile(1 - side, m, v)[at]
                        got = jnp.take_along_axis(face, within, axis=1, mode="promise_in_bounds")
                        picked[v] = got if m == 0 else jnp.where(here, got, picked[v])
                totals = [weight * picked[v] if k == 0 else totals[v] + weight * picked[v] for v in range(NV)]
            parts.append(totals)
        return [jnp.concatenate([parts[0][v], parts[1][v]], axis=0) for v in range(NV)]

    def order_weights(side, level):
        rows = lambda k: table[pl.ds(HALF * side * HALF_ZONE * NT + k * NT + level, HALF, stride=HALF_ZONE * NT), :]
        first = rows(0).astype(jnp.int32)
        within, which = first & (W - 1), first >> 7
        weight = [rows(1 + k) for k in range(4)]
        eight = lax.broadcasted_iota(jnp.int32, (HALF, W), 0)
        many = lax.broadcasted_iota(jnp.int32, (W, W), 0)
        spread, chosen = [], []
        for j in range(HALF):
            here = jnp.broadcast_to(which[j : j + 1], (HALF, W)) == eight
            spread.append(
                jnp.concatenate(
                    [jnp.where(here, jnp.broadcast_to(weight[k][j : j + 1], (HALF, W)), 0.0) for k in range(4)], axis=0
                )
            )
            hit = jnp.broadcast_to(within[j : j + 1], (W, W)) == many
            chosen.append(jnp.where(hit, 1.0, 0.0).astype(jnp.bfloat16))
        spread = jnp.concatenate(spread, axis=1)
        chosen = jnp.concatenate(chosen, axis=1)
        lead = spread.astype(jnp.bfloat16)
        rest = (spread - lead.astype(jnp.float32)).astype(jnp.bfloat16)
        both = lax.dot_general(
            jnp.concatenate([lead, rest], axis=0), chosen, (((1,), (1,)), ((), ())), preferred_element_type=jnp.float32
        )
        both = both[:32] + both[32:]
        for k in range(4):
            ordered[side, k, pl.ds(level, HALF, stride=NT), :] = both[8 * k : 8 * k + 8]

    def step(j, _):
        for side in range(2):
            ghost = interpolate_first(side, j)
            for v in range(NV):
                ghosts[side, v, j] = ghost[v]
            order_weights(side, 2 * j)
            order_weights(side, 2 * j + 1)
        return 0

    lax.fori_loop(0, HALF, step, 0)


def chain(
    low, high, given_ghosts, ordered, matrix, flow, out,
    cur0, cur1, nexts0, nexts1, prevs0, prevs1, shifted, weighed, ghosts, applied,
):
    _, block = place()
    own_side, own = block // HALF, block % HALF
    lane = lax.broadcasted_iota(jnp.int32, (NT, W), 1)
    cur, nexts, prevs = (cur0, cur1), (nexts0, nexts1), (prevs0, prevs1)

    def tile(side, j, k):
        return zone_tile(low, high, side, j, k)

    def value(section, side, line, v, j):
        if section == 0:
            return tile(side, j, line * NV + v)
        return cur[section % 2][side, line, v, j]

    def keep_rolled(section, side, line, v, j, values, shift=False):
        nexts[section % 2][side, line, v, j] = pltpu.roll(values, W - 1, 1)
        prevs[section % 2][side, line, v, j] = pltpu.roll(values, 1, 1)
        if shift:
            shifted[0, side, v, j] = pltpu.roll(values, W - 2, 1)
            shifted[1, side, v, j] = pltpu.roll(values, W - 3, 1)

    def weigh(section, side, m):
        other, after = 1 - side, (m + 1) % HALF
        weight = [ordered[side, k, pl.ds(pl.multiple_of(m * NT, NT), NT), :] for k in range(4)]
        for v in range(NV):
            total = weight[0] * value(section, other, 0, v, m)
            for k in range(1, 4):
                if k == 1:
                    here, there = nexts[section % 2][other, 0, v, m], nexts[section % 2][other, 0, v, after]
                else:
                    here, there = shifted[k - 2, other, v, m], shifted[k - 2, other, v, after]
                total = total + weight[k] * jnp.where(lane >= W - k, there, here)
            weighed[side, v, m] = total

    def interpolate(side, j):
        first = tile(side, j, 20).astype(jnp.int32)
        within, which = first & (W - 1), first >> 7
        parts = []
        for h in range(2):
            at = slice(8 * h, 8 * h + 8)
            picked = [None] * NV
            for m in range(HALF):
                here = which[at] == m
                for v in range(NV):
                    got = jnp.take_along_axis(weighed[side, v, m, at], within[at], axis=1, mode="promise_in_bounds")
                    picked[v] = got if m == 0 else jnp.where(here, got, picked[v])
            parts.append(picked)
        return [jnp.concatenate([parts[0][v], parts[1][v]], axis=0) for v in range(NV)]

    def first_rolls(j, _):
        for side in range(2):
            for line in range(4):
                for v in range(NV):
                    keep_rolled(0, side, line, v, j, value(0, side, line, v, j))
        return 0

    lax.fori_loop(0, HALF, first_rolls, 0)
    for s in range(4):
        sides = (0, 1) if s < 3 else (1 - own_side,)

        def weigh_step(m, _, s=s):
            weigh(s, 0, m)
            weigh(s, 1, m)
            return 0

        def advance(side, j, s=s):
            after, before = (j + 1) % HALF, (j + HALF - 1) % HALF
            coefs = coefficients(flow, side)
            if s == 0:
                ghost = [given_ghosts[side, v, j] for v in range(NV)]
            else:
                ghost = interpolate(side, j)
                for v in range(NV):
                    ghosts[s % 2, side, v, j] = ghost[v]
            lines = 4 - s
            here = [[value(s, side, line, v, j) for v in range(NV)] for line in range(lines + 1)]
            product = level_product(
                matrix[...], jnp.concatenate([jnp.concatenate(here[line], axis=0) for line in range(lines)], axis=1)
            )
            for line in reversed(range(lines)):
                up = ghost if line == 0 else here[line - 1]
                nxt = [
                    jnp.where(lane == W - 1, nexts[s % 2][side, line, v, after], nexts[s % 2][side, line, v, j])
                    for v in range(NV)
                ]
                prv = [
                    jnp.where(lane == 0, prevs[s % 2][side, line, v, before], prevs[s % 2][side, line, v, j])
                    for v in range(NV)
                ]
                timed = split(product[:, line * W : (line + 1) * W])
                rate = rates(coefs, up, here[line + 1], nxt, prv, timed)
                for v in range(NV):
                    result = value(0, side, line, v, j) - SECTION_FACTORS[s] * rate[v]
                    cur[(s + 1) % 2][side, line, v, j] = result
                    if line < max(lines - 1, 1):
                        keep_rolled(s + 1, side, line, v, j, result, line == 0)
        def section_step(j, _, advance=advance, sides=sides):
            for side in sides:
                advance(side, j)
            return 0

        if s > 0:
            lax.fori_loop(0, HALF, weigh_step, 0, unroll=2)
        lax.fori_loop(0, HALF, section_step, 0, unroll=SU[s])
        if s == 3:

            def own_step(step, _):
                j = (own + HALF - 1 + step) % HALF
                ghost = interpolate(own_side, j)
                for v in range(NV):
                    ghosts[1, own_side, v, j] = ghost[v]
                return 0

            lax.fori_loop(0, 3, own_step, 0)
        kept = given_ghosts if s == 0 else ghosts.at[s % 2]
        for v in range(NV):
            at = slice(v * NT, (v + 1) * NT)
            applied[s, at, :W] = kept[own_side, v, own]
            after = kept[own_side, v, (own + 1) % HALF]
            before = kept[own_side, v, (own + HALF - 1) % HALF]
            applied[s, at, W:] = jnp.where(lane < W // 2, after, before)

    def last_weigh(m, _):
        weigh(4, own_side, m)
        return 0

    lax.fori_loop(0, HALF, last_weigh, 0, unroll=4)
    got = interpolate(own_side, own)
    for v in range(NV):
        at = slice(v * NT, (v + 1) * NT)
        applied[4, at, :W] = got[v]
        applied[4, at, W:] = got[v]

    coefs = coefficients(flow, own_side)
    zero = jnp.zeros((NV * NT, 2 * W), jnp.float32)
    response = []
    for s in range(5):
        product = None
        if s:
            product = level_product(matrix[...], jnp.concatenate(response, axis=1))
        padded = [applied[s]] + response + [zero, zero]
        new = []
        for line in range(s + 1):
            here = padded[line + 1]
            if line < s:
                nxt, prv = pltpu.roll(here, 2 * W - 1, 1), pltpu.roll(here, 1, 1)
                timed = product[:, 2 * W * line : 2 * W * (line + 1)]
            else:
                nxt = prv = timed = zero
            rate = rates(coefs, split(padded[line]), split(padded[line + 2]), split(nxt), split(prv), split(timed))
            new.append(-SECTION_FACTORS[s] * jnp.concatenate(rate, axis=0))
        response = new

    for line in range(HALO):
        for v in range(NV):
            cell = jnp.where(own_side == 0, HALO - 1 - line, line)
            out[pl.ds(v * ROW + cell, NT, stride=NR), :] = response[line][v * NT : (v + 1) * NT, :W]


def bulk(lines, below, above, from_left, from_right, matrix, flow, out, start, even, odd):
    t, block = place()
    side = block // HALF
    lane = lax.broadcasted_iota(jnp.int32, (NT, W), 1)
    for m in range(LINES * NV):
        r, v = m // NV - HALO, m % NV
        at = slice(v * NT, (v + 1) * NT)
        start[m // NV, at, :W] = line_tile(lines, below, above, t, side, r, v)
        p, k = m // 16, m % 16
        after = from_right[p * NT : (p + 1) * NT]
        after = after if k == 0 else pltpu.roll(after, W - 8 * k, 1)
        before = from_left[p * NT : (p + 1) * NT]
        before = before if k == 15 else pltpu.roll(before, 120 - 8 * k, 1)
        start[m // NV, at, W:] = jnp.where(lane < W // 2, after, before)
    coefs = coefficients(flow, side)
    group = 4
    for s in range(5):
        now = start if s == 0 else (even if s % 2 == 0 else odd)
        new = odd if s % 2 == 0 else even

        @pl.when(t == PARTS - 1)
        def _(now=now):
            now[HALO + TAIL] = jnp.zeros((NV * NT, 2 * W), jnp.float32)

        if s > 0:

            @pl.when(t == 0)
            def _(now=now):
                now[HALO - 1] = start[HALO - 1]

        first = (1, 1, 3, 3, 5)[s]

        def line_step(step, _, now=now, new=new, s=s, first=first):
            i = first + group * step
            here = [now[i - 1 + g] for g in range(group + 2)]
            product = level_product(matrix[...], jnp.concatenate(here[1:-1], axis=1))
            for g in range(group):
                line = here[g + 1]
                nxt = pltpu.roll(line, 2 * W - 1, 1)
                prv = pltpu.roll(line, 1, 1)
                timed = split(product[:, 2 * W * g : 2 * W * (g + 1)])
                rate = rates(coefs, split(here[g + 2]), split(here[g]), split(nxt), split(prv), timed)
                base = split(start[i + g])
                for v in range(NV):
                    result = base[v] - SECTION_FACTORS[s] * rate[v]
                    if s < 4:
                        new[i + g, v * NT : (v + 1) * NT] = result
                    else:
                        cell = jnp.where(side == 0, i + g - HALO, CHUNK + HALO - i - g)
                        out[pl.ds(v * ROW + cell, NT, stride=NR), :] = result[:, :W]
            return 0

        lax.fori_loop(0, (LINES - 2 * first + group - 1) // group, line_step, 0)


def main_kernel(
    low, high, given_ghosts, ordered, lines, below, above, from_left, from_right, matrix, flow, out, *scratch
):
    t, _ = place()

    @pl.when(t < PARTS)
    def _():
        bulk(lines, below, above, from_left, from_right, matrix, flow, out, *scratch[:3])

    @pl.when(t >= PARTS)
    def _():
        chain(low, high, given_ghosts, ordered, matrix, flow, out, *scratch[3:])


def unpack_kernel(shares, out):
    _, block = place()

    def fill(rotor):
        for t in range(PARTS):
            first = t * CHUNK if rotor else 256 - (t + 1) * CHUNK
            skip = max(-first, 0)
            count = min(CHUNK, 256 - first) - skip
            for v in range(NV):
                at = v * ROW + skip + (0 if rotor else 1)
                share = shares[t, at : at + count]
                if t == PARTS - 1:
                    added = shares[NT - 1, v * ROW : v * ROW + HALO]
                    none = jnp.zeros((count - HALO, W), jnp.float32)
                    share = share + jnp.concatenate([none, added] if rotor else [added, none], axis=0)
                out[v, first + skip : first + skip + count] = share

    @pl.when(block < HALF)
    def _():
        fill(True)

    @pl.when(block >= HALF)
    def _():
        fill(False)


def f32(*shape):
    return jax.ShapeDtypeStruct(shape, jnp.float32)


def cost(flops, nbytes):
    return pl.CostEstimate(flops=flops, bytes_accessed=nbytes, transcendentals=0)


def shards(state, far_field, face_index, face_weight, mean_flow):
    matrix = jnp.asarray(level_matrix())
    shares = pl.pallas_call(
        pack_kernel,
        out_shape=f32(NT, NR, W),
        in_specs=[pl.BlockSpec(memory_space=pltpu.HBM)] * 4,
        out_specs=VMEM,
        scratch_shapes=[
            pltpu.VMEM((NV, 256, W), jnp.float32),
            pltpu.VMEM((NV, W), jnp.float32),
            pltpu.VMEM((1, W), jnp.int32),
            pltpu.VMEM((NV, W), jnp.float32),
            pltpu.SemaphoreType.DMA((4,)),
        ],
        compiler_params=params(16),
        name="pack",
    )(state[0], far_field[0], face_index, face_weight[0])
    lines = lax.all_to_all(shares, "tm", 0, 0, tiled=True).reshape(NT * NR, W)
    zone, ends_up, ends_down = pl.pallas_call(
        zone_kernel,
        out_shape=[f32(BLOCKS, HALF_ZONE * NT, W)] + [f32(ENDS * NT, W)] * 2,
        in_specs=[VMEM],
        out_specs=[VMEM] * 3,
        compiler_params=params(16),
        name="zone",
    )(lines)
    high = lax.all_to_all(zone, "block", 0, 0, tiled=True)
    below = lax.ppermute(ends_up, "tm", [(i, i + 1) for i in range(PARTS - 1)])
    above = lax.ppermute(ends_down, "tm", [(i + 1, i) for i in range(PARTS - 1)])
    left, right = pl.pallas_call(
        edge_kernel,
        out_shape=[f32(EDGE_PACKS * NT, W)] * 2,
        in_specs=[VMEM] * 3,
        out_specs=[VMEM] * 2,
        compiler_params=params(16),
        name="edges",
    )(lines, below, above)
    rights = [
        (i * BLOCKS + b, i * BLOCKS + b // HALF * HALF + (b + 1) % HALF) for i in range(PARTS) for b in range(BLOCKS)
    ]
    from_left = lax.ppermute(right, ("tm", "block"), rights)
    from_right = lax.ppermute(left, ("tm", "block"), [(b, a) for a, b in rights])
    high, from_left, from_right = lax.optimization_barrier((high, from_left, from_right))
    low = lax.ppermute(high, "tm", [(PARTS, PARTS + 1)])
    given_ghosts, ordered = pl.pallas_call(
        start_kernel,
        out_shape=[f32(2, NV, HALF, NT, W), f32(2, 4, HALF * NT, W)],
        in_specs=[VMEM] * 2,
        out_specs=[VMEM] * 2,
        compiler_params=params(16),
        cost_estimate=cost(4 * 10**9, 16 << 20),
        name="start",
    )(high, high.reshape(BLOCKS * HALF_ZONE * NT, W))
    grid = pltpu.VMEM((LINES + 3, NV * NT, 2 * W), jnp.float32)
    lines_of = pltpu.VMEM((2, 4, NV, HALF, NT, W), jnp.float32)
    faces_of = pltpu.VMEM((2, 2, NV, HALF, NT, W), jnp.float32)
    done = pl.pallas_call(
        main_kernel,
        out_shape=f32(NT * NR, W),
        in_specs=[VMEM] * 10 + [SMEM],
        out_specs=VMEM,
        scratch_shapes=[grid] * 3
        + [lines_of] * 6
        + [faces_of, pltpu.VMEM((2, NV, HALF, NT, W), jnp.float32)]
        + [faces_of, pltpu.VMEM((5, NV * NT, 2 * W), jnp.float32)],
        compiler_params=params(32),
        cost_estimate=cost(8 * 10**9, 64 << 20),
        name="main",
    )(low, high, given_ghosts, ordered, lines, below, above, from_left, from_right, matrix, mean_flow)
    done = lax.all_to_all(done.reshape(NT, NR, W), "tm", 0, 0, tiled=True)
    result = pl.pallas_call(
        unpack_kernel,
        out_shape=f32(NV, 256, W),
        in_specs=[VMEM],
        out_specs=VMEM,
        compiler_params=params(16),
        name="unpack",
    )(done)
    return result[None]


def solution(mesh):
    in_specs = (
        P("tm", None, None, "block"),
        P("tm", None, "block"),
        P("tm", "block"),
        P("tm", None, "block"),
        P(),
    )
    out_specs = P("tm", None, None, "block")
    return jax.shard_map(shards, mesh=mesh, in_specs=in_specs, out_specs=out_specs, check_vma=False)
```

```python
import jax
import jax.numpy as jnp
import ml_dtypes
import numpy as np
from jax import lax
from jax.experimental import pallas as pl
from jax.experimental.pallas import tpu as pltpu
from jax.sharding import PartitionSpec as P

SECTION_FACTORS = (0.075, 0.05, 0.1125, 0.15, 0.3)
OMEGA = 1.0
DISSIPATION = 0.2

NT = 16
NV = 4
PARTS = 14
CHUNK = 19
HALO = 5
LINES = CHUNK + 2 * HALO
TAIL = 256 - (PARTS - 1) * CHUNK
W = 128
HALF = 8
BLOCKS = 16
NR = 80
ROW = 20
HALF_ZONE = 13
ENDS = HALO * NV
EDGE_PACKS = 8
FIRST_HALF = tuple(range(4, 17))
SECOND_HALF = (20, 21, 22, 23, 24, 0, 1, 2, 3, 17, 18, 19)
SU = (1, 2, 2, 4)
VMEM = pl.BlockSpec(memory_space=pltpu.VMEM)
HBM = pl.BlockSpec(memory_space=pltpu.HBM)
SMEM = pl.BlockSpec(memory_space=pltpu.SMEM)


def level_matrix():
    offsets = np.arange(NT)[:, None] - np.arange(NT)[None, :]
    angle = np.pi * offsets / NT
    safe = np.where(offsets == 0, 0.5 * np.pi, angle)
    cot = np.cos(safe) / np.sin(safe)
    matrix = np.where(offsets == 0, 0.0, 0.5 * (1.0 - 2.0 * (offsets % 2)) * cot)
    matrix = OMEGA * matrix + 4.0 * DISSIPATION * np.eye(NT)
    matrix = np.kron(np.eye(NV), matrix).astype(np.float32)
    lead = matrix.astype(ml_dtypes.bfloat16)
    rest = (matrix - lead.astype(np.float32)).astype(ml_dtypes.bfloat16)
    return np.concatenate([lead, rest, lead], axis=1)


def params(mib):
    return pltpu.CompilerParams(vmem_limit_bytes=mib << 20)


def place():
    return lax.axis_index("tm"), lax.axis_index("block")


def pack_kernel(state_in, far_in, index_in, weight_in, out, state, far, index, weight, sems):
    copies = [
        pltpu.make_async_copy(source, target, sems.at[i])
        for i, (source, target) in enumerate(
            ((state_in, state), (far_in, far), (index_in, index), (weight_in, weight))
        )
    ]
    for copy in copies:
        copy.start()
    for copy in copies:
        copy.wait()
    _, block = place()

    def fill(rotor):
        for t in range(PARTS):
            first = t * CHUNK if rotor else 256 - (t + 1) * CHUNK
            skip = max(-first, 0)
            count = min(CHUNK, 256 - first) - skip
            for v in range(NV):
                at = v * ROW + skip
                out[t, at : at + count] = state[v, first + skip : first + skip + count]
                out[t, v * ROW + CHUNK : (v + 1) * ROW] = far[v : v + 1]
        lines = []
        for line in range(HALO):
            cell = 255 - line if rotor else line
            lines += [state[v, cell : cell + 1] for v in range(NV)]
        lines += [index[...].astype(jnp.float32)] + [weight[k : k + 1] for k in range(4)]
        for t, half in ((PARTS, FIRST_HALF), (PARTS + 1, SECOND_HALF)):
            for i, k in enumerate(half):
                out[t, i : i + 1] = lines[k]

    @pl.when(block < HALF)
    def _():
        fill(True)

    @pl.when(block >= HALF)
    def _():
        fill(False)


def line_address(side, r, v):
    return v * ROW + jnp.where(side == 0, r, CHUNK - 1 - r)


def zone_kernel(lines, zone, ends_up, ends_down):
    _, block = place()
    side = block // HALF
    for i in range(HALF_ZONE):
        tile = lines[pl.ds(i, NT, stride=NR), :]
        for b in range(BLOCKS):
            zone[b, i * NT : (i + 1) * NT] = tile
    for i in range(ENDS):
        r, v = i // NV, i % NV
        at = slice(i * NT, (i + 1) * NT)
        ends_up[at] = lines[pl.ds(line_address(side, CHUNK - HALO + r, v), NT, stride=NR), :]
        ends_down[at] = lines[pl.ds(line_address(side, r, v), NT, stride=NR), :]


def line_tile(lines, below, above, t, side, r, v):
    if r < 0:
        at = (r + HALO) * NV + v
        tile = below[at * NT : (at + 1) * NT]
        if r == -1:
            tile = jnp.where(t == 0, lines[pl.ds(v * ROW + CHUNK, NT, stride=NR), :], tile)
        return tile
    if r < CHUNK:
        return lines[pl.ds(line_address(side, r, v), NT, stride=NR), :]
    at = (r - CHUNK) * NV + v
    return above[at * NT : (at + 1) * NT]


def edge_kernel(lines, below, above, left, right):
    t, block = place()
    side = block // HALF
    part = lax.broadcasted_iota(jnp.int32, (NT, W), 1) // 8
    for p in range(EDGE_PACKS):
        left_pack = jnp.zeros((NT, W), jnp.float32)
        right_pack = jnp.zeros((NT, W), jnp.float32)
        for k in range(16):
            m = p * 16 + k
            if m >= LINES * NV:
                break
            tile = line_tile(lines, below, above, t, side, m // NV - HALO, m % NV)
            moved = tile if k == 0 else pltpu.roll(tile, 8 * k, 1)
            left_pack = jnp.where(part == k, moved, left_pack)
            moved = tile if k == 15 else pltpu.roll(tile, 8 * k + 8, 1)
            right_pack = jnp.where(part == k, moved, right_pack)
        left[p * NT : (p + 1) * NT] = left_pack
        right[p * NT : (p + 1) * NT] = right_pack


def coefficients(flow, side):
    sign = (0.5, -0.5)[side] if isinstance(side, int) else jnp.where(side == 0, 0.5, -0.5)
    along = sign * flow[side, 0]
    across = 0.5 * flow[side, 1]
    return sign, along - DISSIPATION, -along - DISSIPATION, across - DISSIPATION, -across - DISSIPATION


def rates(coefs, up, down, nxt, prv, timed):
    sign, cu, cd, cn, cp = coefs
    plain = [timed[v] + (cu * up[v] + cd * down[v]) + (cn * nxt[v] + cp * prv[v]) for v in range(NV)]
    mixed = sign * (up[1] - down[1]) + 0.5 * (nxt[2] - prv[2])
    pressure_up = sign * (up[3] - down[3])
    pressure_next = 0.5 * (nxt[3] - prv[3])
    return [plain[0] + mixed, plain[1] + pressure_up, plain[2] + pressure_next, plain[3] + mixed]


def level_product(matrix, values):
    lead = values.astype(jnp.bfloat16)
    rest = (values - lead.astype(jnp.float32)).astype(jnp.bfloat16)
    return jnp.dot(matrix, jnp.concatenate([lead, lead, rest], axis=0), preferred_element_type=jnp.float32)


def split(lines):
    return [lines[v * NT : (v + 1) * NT] for v in range(NV)]


def zone_tile(first_half, second_half, side, j, k):
    source, at = (first_half, FIRST_HALF.index(k)) if k in FIRST_HALF else (second_half, SECOND_HALF.index(k))
    return source[HALF * side + j, at * NT : (at + 1) * NT, :]


def start_kernel(high, table, ghosts, ordered):
    def tile(side, j, k):
        return zone_tile(None, high, side, j, k)

    def interpolate_first(side, j):
        first = tile(side, j, 20).astype(jnp.int32)
        parts = []
        for h in range(2):
            at = slice(8 * h, 8 * h + 8)
            totals = [None] * NV
            for k in range(4):
                source = (first[at] + k) & (HALF * W - 1)
                within, which = source & (W - 1), source >> 7
                weight = tile(side, j, 21 + k)[at]
                picked = [None] * NV
                for m in range(HALF):
                    here = which == m
                    for v in range(NV):
                        face = tile(1 - side, m, v)[at]
                        got = jnp.take_along_axis(face, within, axis=1, mode="promise_in_bounds")
                        picked[v] = got if m == 0 else jnp.where(here, got, picked[v])
                totals = [weight * picked[v] if k == 0 else totals[v] + weight * picked[v] for v in range(NV)]
            parts.append(totals)
        return [jnp.concatenate([parts[0][v], parts[1][v]], axis=0) for v in range(NV)]

    def order_weights(side, level):
        rows = lambda k: table[pl.ds(HALF * side * HALF_ZONE * NT + k * NT + level, HALF, stride=HALF_ZONE * NT), :]
        first = rows(0).astype(jnp.int32)
        within, which = first & (W - 1), first >> 7
        weight = [rows(1 + k) for k in range(4)]
        eight = lax.broadcasted_iota(jnp.int32, (HALF, W), 0)
        many = lax.broadcasted_iota(jnp.int32, (W, W), 0)
        spread, chosen = [], []
        for j in range(HALF):
            here = jnp.broadcast_to(which[j : j + 1], (HALF, W)) == eight
            spread.append(
                jnp.concatenate(
                    [jnp.where(here, jnp.broadcast_to(weight[k][j : j + 1], (HALF, W)), 0.0) for k in range(4)], axis=0
                )
            )
            hit = jnp.broadcast_to(within[j : j + 1], (W, W)) == many
            chosen.append(jnp.where(hit, 1.0, 0.0).astype(jnp.bfloat16))
        spread = jnp.concatenate(spread, axis=1)
        chosen = jnp.concatenate(chosen, axis=1)
        lead = spread.astype(jnp.bfloat16)
        rest = (spread - lead.astype(jnp.float32)).astype(jnp.bfloat16)
        both = lax.dot_general(
            jnp.concatenate([lead, rest], axis=0), chosen, (((1,), (1,)), ((), ())), preferred_element_type=jnp.float32
        )
        both = both[:32] + both[32:]
        for k in range(4):
            ordered[side, k, pl.ds(level, HALF, stride=NT), :] = both[8 * k : 8 * k + 8]

    def step(j, _):
        for side in range(2):
            ghost = interpolate_first(side, j)
            for v in range(NV):
                ghosts[side, v, j] = ghost[v]
            order_weights(side, 2 * j)
            order_weights(side, 2 * j + 1)
        return 0

    @pl.when(place()[0] >= PARTS)
    def _():
        lax.fori_loop(0, HALF, step, 0)


def chain(
    low, high, given_ghosts, ordered, matrix, flow, out,
    cur0, cur1, nexts0, nexts1, prevs0, prevs1, shifted, weighed, ghosts, applied,
):
    _, block = place()
    own_side, own = block // HALF, block % HALF
    lane = lax.broadcasted_iota(jnp.int32, (NT, W), 1)
    cur, nexts, prevs = (cur0, cur1), (nexts0, nexts1), (prevs0, prevs1)

    def tile(side, j, k):
        return zone_tile(low, high, side, j, k)

    def value(section, side, line, v, j):
        if section == 0:
            return tile(side, j, line * NV + v)
        return cur[section % 2][side, line, v, j]

    def keep_rolled(section, side, line, v, j, values, shift=False):
        nexts[section % 2][side, line, v, j] = pltpu.roll(values, W - 1, 1)
        prevs[section % 2][side, line, v, j] = pltpu.roll(values, 1, 1)
        if shift:
            shifted[0, side, v, j] = pltpu.roll(values, W - 2, 1)
            shifted[1, side, v, j] = pltpu.roll(values, W - 3, 1)

    def weigh(section, side, m):
        other, after = 1 - side, (m + 1) % HALF
        weight = [ordered[side, k, pl.ds(pl.multiple_of(m * NT, NT), NT), :] for k in range(4)]
        for v in range(NV):
            total = weight[0] * value(section, other, 0, v, m)
            for k in range(1, 4):
                if k == 1:
                    here, there = nexts[section % 2][other, 0, v, m], nexts[section % 2][other, 0, v, after]
                else:
                    here, there = shifted[k - 2, other, v, m], shifted[k - 2, other, v, after]
                total = total + weight[k] * jnp.where(lane >= W - k, there, here)
            weighed[side, v, m] = total

    def interpolate(side, j):
        first = tile(side, j, 20).astype(jnp.int32)
        within, which = first & (W - 1), first >> 7
        parts = []
        for h in range(2):
            at = slice(8 * h, 8 * h + 8)
            picked = [None] * NV
            for m in range(HALF):
                here = which[at] == m
                for v in range(NV):
                    got = jnp.take_along_axis(weighed[side, v, m, at], within[at], axis=1, mode="promise_in_bounds")
                    picked[v] = got if m == 0 else jnp.where(here, got, picked[v])
            parts.append(picked)
        return [jnp.concatenate([parts[0][v], parts[1][v]], axis=0) for v in range(NV)]

    for s in range(4):
        sides = (0, 1) if s < 3 else (1 - own_side,)

        def weigh_step(m, _, s=s):
            weigh(s, 0, m)
            weigh(s, 1, m)
            return 0

        def advance(side, j, s=s):
            after, before = (j + 1) % HALF, (j + HALF - 1) % HALF
            coefs = coefficients(flow, side)
            if s == 0:
                ghost = [given_ghosts[side, v, j] for v in range(NV)]
            else:
                ghost = interpolate(side, j)
                for v in range(NV):
                    ghosts[s % 2, side, v, j] = ghost[v]
            lines = 4 - s
            here = [[value(s, side, line, v, j) for v in range(NV)] for line in range(lines + 1)]
            product = level_product(
                matrix[...], jnp.concatenate([jnp.concatenate(here[line], axis=0) for line in range(lines)], axis=1)
            )
            for line in reversed(range(lines)):
                up = ghost if line == 0 else here[line - 1]
                nxt, prv = [], []
                for v in range(NV):
                    if s == 0:
                        ahead = jnp.where(lane == 0, value(0, side, line, v, after), here[line][v])
                        behind = jnp.where(lane == W - 1, value(0, side, line, v, before), here[line][v])
                        nxt.append(pltpu.roll(ahead, W - 1, 1))
                        prv.append(pltpu.roll(behind, 1, 1))
                    else:
                        ahead, behind = nexts[s % 2], prevs[s % 2]
                        nxt.append(jnp.where(lane == W - 1, ahead[side, line, v, after], ahead[side, line, v, j]))
                        prv.append(jnp.where(lane == 0, behind[side, line, v, before], behind[side, line, v, j]))
                timed = split(product[:, line * W : (line + 1) * W])
                rate = rates(coefs, up, here[line + 1], nxt, prv, timed)
                for v in range(NV):
                    result = value(0, side, line, v, j) - SECTION_FACTORS[s] * rate[v]
                    cur[(s + 1) % 2][side, line, v, j] = result
                    if line < max(lines - 1, 1):
                        keep_rolled(s + 1, side, line, v, j, result, line == 0)
        def section_step(j, _, advance=advance, sides=sides):
            for side in sides:
                advance(side, j)
            return 0

        if s > 0:
            lax.fori_loop(0, HALF, weigh_step, 0, unroll=2)
        lax.fori_loop(0, HALF, section_step, 0, unroll=SU[s])
        if s == 3:

            def own_step(step, _):
                j = (own + HALF - 1 + step) % HALF
                ghost = interpolate(own_side, j)
                for v in range(NV):
                    ghosts[1, own_side, v, j] = ghost[v]
                return 0

            lax.fori_loop(0, 3, own_step, 0)
        kept = given_ghosts if s == 0 else ghosts.at[s % 2]
        for v in range(NV):
            at = slice(v * NT, (v + 1) * NT)
            applied[s, at, :W] = kept[own_side, v, own]
            after = kept[own_side, v, (own + 1) % HALF]
            before = kept[own_side, v, (own + HALF - 1) % HALF]
            applied[s, at, W:] = jnp.where(lane < W // 2, after, before)

    def last_weigh(m, _):
        weigh(4, own_side, m)
        return 0

    lax.fori_loop(0, HALF, last_weigh, 0, unroll=4)
    got = interpolate(own_side, own)
    for v in range(NV):
        at = slice(v * NT, (v + 1) * NT)
        applied[4, at, :W] = got[v]
        applied[4, at, W:] = got[v]

    coefs = coefficients(flow, own_side)
    zero = jnp.zeros((NV * NT, 2 * W), jnp.float32)
    response = []
    for s in range(5):
        product = None
        if s:
            product = level_product(matrix[...], jnp.concatenate(response, axis=1))
        padded = [applied[s]] + response + [zero, zero]
        new = []
        for line in range(s + 1):
            here = padded[line + 1]
            if line < s:
                nxt, prv = pltpu.roll(here, 2 * W - 1, 1), pltpu.roll(here, 1, 1)
                timed = product[:, 2 * W * line : 2 * W * (line + 1)]
            else:
                nxt = prv = timed = zero
            rate = rates(coefs, split(padded[line]), split(padded[line + 2]), split(nxt), split(prv), split(timed))
            new.append(-SECTION_FACTORS[s] * jnp.concatenate(rate, axis=0))
        response = new

    for line in range(HALO):
        for v in range(NV):
            cell = jnp.where(own_side == 0, HALO - 1 - line, line)
            out[pl.ds(v * ROW + cell, NT, stride=NR), :] = response[line][v * NT : (v + 1) * NT, :W]


def bulk(lines, below, above, from_left, from_right, matrix, flow, out, start, even, odd):
    t, block = place()
    side = block // HALF
    lane = lax.broadcasted_iota(jnp.int32, (NT, W), 1)
    for m in range(LINES * NV):
        r, v = m // NV - HALO, m % NV
        at = slice(v * NT, (v + 1) * NT)
        start[m // NV, at, :W] = line_tile(lines, below, above, t, side, r, v)
        p, k = m // 16, m % 16
        after = from_right[p * NT : (p + 1) * NT]
        after = after if k == 0 else pltpu.roll(after, W - 8 * k, 1)
        before = from_left[p * NT : (p + 1) * NT]
        before = before if k == 15 else pltpu.roll(before, 120 - 8 * k, 1)
        start[m // NV, at, W:] = jnp.where(lane < W // 2, after, before)
    coefs = coefficients(flow, side)
    group = 4
    for s in range(5):
        now = start if s == 0 else (even if s % 2 == 0 else odd)
        new = odd if s % 2 == 0 else even

        @pl.when(t == PARTS - 1)
        def _(now=now):
            now[HALO + TAIL] = jnp.zeros((NV * NT, 2 * W), jnp.float32)

        if s > 0:

            @pl.when(t == 0)
            def _(now=now):
                now[HALO - 1] = start[HALO - 1]

        first = (1, 1, 3, 3, 5)[s]

        def line_step(step, _, now=now, new=new, s=s, first=first):
            i = first + group * step
            here = [now[i - 1 + g] for g in range(group + 2)]
            product = level_product(matrix[...], jnp.concatenate(here[1:-1], axis=1))
            for g in range(group):
                line = here[g + 1]
                nxt = pltpu.roll(line, 2 * W - 1, 1)
                prv = pltpu.roll(line, 1, 1)
                timed = split(product[:, 2 * W * g : 2 * W * (g + 1)])
                rate = rates(coefs, split(here[g + 2]), split(here[g]), split(nxt), split(prv), timed)
                base = split(start[i + g])
                for v in range(NV):
                    result = base[v] - SECTION_FACTORS[s] * rate[v]
                    if s < 4:
                        new[i + g, v * NT : (v + 1) * NT] = result
                    else:
                        cell = jnp.where(side == 0, i + g - HALO, CHUNK + HALO - i - g)
                        out[pl.ds(v * ROW + cell, NT, stride=NR), :] = result[:, :W]
            return 0

        lax.fori_loop(0, (LINES - 2 * first + group - 1) // group, line_step, 0)


def main_kernel(
    low, high, given_ghosts, ordered, lines, below, above, from_left, from_right, matrix, flow, out, *scratch
):
    t, _ = place()

    @pl.when(t < PARTS)
    def _():
        bulk(lines, below, above, from_left, from_right, matrix, flow, out, *scratch[:3])

    @pl.when(t >= PARTS)
    def _():
        chain(low, high, given_ghosts, ordered, matrix, flow, out, *scratch[3:])


def unpack_kernel(shares, out):
    _, block = place()

    def fill(rotor):
        for t in range(PARTS):
            first = t * CHUNK if rotor else 256 - (t + 1) * CHUNK
            skip = max(-first, 0)
            count = min(CHUNK, 256 - first) - skip
            for v in range(NV):
                at = v * ROW + skip + (0 if rotor else 1)
                share = shares[t, at : at + count]
                if t == PARTS - 1:
                    added = shares[NT - 1, v * ROW : v * ROW + HALO]
                    none = jnp.zeros((count - HALO, W), jnp.float32)
                    share = share + jnp.concatenate([none, added] if rotor else [added, none], axis=0)
                out[v, first + skip : first + skip + count] = share

    @pl.when(block < HALF)
    def _():
        fill(True)

    @pl.when(block >= HALF)
    def _():
        fill(False)


def f32(*shape):
    return jax.ShapeDtypeStruct(shape, jnp.float32)


def cost(flops, nbytes):
    return pl.CostEstimate(flops=flops, bytes_accessed=nbytes, transcendentals=0)


def shards(state, far_field, face_index, face_weight, mean_flow):
    matrix = jnp.asarray(level_matrix())
    shares = pl.pallas_call(
        pack_kernel,
        out_shape=f32(NT, NR, W),
        in_specs=[HBM] * 4,
        out_specs=VMEM,
        scratch_shapes=[
            pltpu.VMEM((NV, 256, W), jnp.float32),
            pltpu.VMEM((NV, W), jnp.float32),
            pltpu.VMEM((1, W), jnp.int32),
            pltpu.VMEM((NV, W), jnp.float32),
            pltpu.SemaphoreType.DMA((4,)),
        ],
        compiler_params=params(60),
        name="pack",
    )(state[0], far_field[0], face_index, face_weight[0])
    lines = lax.all_to_all(shares, "tm", 0, 0, tiled=True).reshape(NT * NR, W)
    zone, ends_up, ends_down = pl.pallas_call(
        zone_kernel,
        out_shape=[f32(BLOCKS, HALF_ZONE * NT, W)] + [f32(ENDS * NT, W)] * 2,
        in_specs=[VMEM],
        out_specs=[VMEM] * 3,
        compiler_params=params(16),
        name="zone",
    )(lines)
    high = lax.all_to_all(zone, "block", 0, 0, tiled=True)
    below = lax.ppermute(ends_up, "tm", [(i, i + 1) for i in range(PARTS - 1)])
    above = lax.ppermute(ends_down, "tm", [(i + 1, i) for i in range(PARTS - 1)])
    left, right = pl.pallas_call(
        edge_kernel,
        out_shape=[f32(EDGE_PACKS * NT, W)] * 2,
        in_specs=[VMEM] * 3,
        out_specs=[VMEM] * 2,
        compiler_params=params(16),
        name="edges",
    )(lines, below, above)
    rights = [
        (i * BLOCKS + b, i * BLOCKS + b // HALF * HALF + (b + 1) % HALF) for i in range(PARTS) for b in range(BLOCKS)
    ]
    from_left = lax.ppermute(right, ("tm", "block"), rights)
    from_right = lax.ppermute(left, ("tm", "block"), [(b, a) for a, b in rights])
    high, from_left, from_right = lax.optimization_barrier((high, from_left, from_right))
    low = lax.ppermute(high, "tm", [(PARTS, PARTS + 1)])
    given_ghosts, ordered = pl.pallas_call(
        start_kernel,
        out_shape=[f32(2, NV, HALF, NT, W), f32(2, 4, HALF * NT, W)],
        in_specs=[VMEM] * 2,
        out_specs=[VMEM] * 2,
        compiler_params=params(16),
        cost_estimate=cost(4 * 10**9, 16 << 20),
        name="start",
    )(high, high.reshape(BLOCKS * HALF_ZONE * NT, W))
    grid = pltpu.VMEM((LINES + 3, NV * NT, 2 * W), jnp.float32)
    lines_of = pltpu.VMEM((2, 4, NV, HALF, NT, W), jnp.float32)
    faces_of = pltpu.VMEM((2, 2, NV, HALF, NT, W), jnp.float32)
    done = pl.pallas_call(
        main_kernel,
        out_shape=f32(NT * NR, W),
        in_specs=[VMEM] * 10 + [SMEM],
        out_specs=VMEM,
        scratch_shapes=[grid] * 3
        + [lines_of] * 6
        + [faces_of, pltpu.VMEM((2, NV, HALF, NT, W), jnp.float32)]
        + [faces_of, pltpu.VMEM((5, NV * NT, 2 * W), jnp.float32)],
        compiler_params=params(32),
        cost_estimate=cost(8 * 10**9, 64 << 20),
        name="main",
    )(low, high, given_ghosts, ordered, lines, below, above, from_left, from_right, matrix, mean_flow)
    done = lax.all_to_all(done.reshape(NT, NR, W), "tm", 0, 0, tiled=True)
    result = pl.pallas_call(
        unpack_kernel,
        out_shape=f32(NV, 256, W),
        in_specs=[VMEM],
        out_specs=VMEM,
        compiler_params=params(16),
        name="unpack",
    )(done)
    return result[None]


def solution(mesh):
    in_specs = (
        P("tm", None, None, "block"),
        P("tm", None, "block"),
        P("tm", "block"),
        P("tm", None, "block"),
        P(),
    )
    out_specs = P("tm", None, None, "block")
    return jax.shard_map(shards, mesh=mesh, in_specs=in_specs, out_specs=out_specs, check_vma=False)
```

```python
import jax
import jax.numpy as jnp
import ml_dtypes
import numpy as np
from jax import lax
from jax.experimental import pallas as pl
from jax.experimental.pallas import tpu as pltpu
from jax.sharding import PartitionSpec as P

SECTION_FACTORS = (0.075, 0.05, 0.1125, 0.15, 0.3)
OMEGA = 1.0
DISSIPATION = 0.2

NT = 16
NV = 4
PARTS = 14
CHUNK = 19
HALO = 5
LINES = CHUNK + 2 * HALO
TAIL = 256 - (PARTS - 1) * CHUNK
W = 128
HALF = 8
BLOCKS = 16
NR = 80
ROW = 20
HALF_ZONE = 13
ENDS = HALO * NV
EDGE_PACKS = 8
FIRST_HALF = tuple(range(4, 17))
SECOND_HALF = (20, 21, 22, 23, 24, 0, 1, 2, 3, 17, 18, 19)
SU = (2, 4, 4, 8)
VMEM = pl.BlockSpec(memory_space=pltpu.VMEM)
HBM = pl.BlockSpec(memory_space=pltpu.HBM)
SMEM = pl.BlockSpec(memory_space=pltpu.SMEM)


def level_matrix():
    offsets = np.arange(NT)[:, None] - np.arange(NT)[None, :]
    angle = np.pi * offsets / NT
    safe = np.where(offsets == 0, 0.5 * np.pi, angle)
    cot = np.cos(safe) / np.sin(safe)
    matrix = np.where(offsets == 0, 0.0, 0.5 * (1.0 - 2.0 * (offsets % 2)) * cot)
    matrix = OMEGA * matrix + 4.0 * DISSIPATION * np.eye(NT)
    matrix = np.asarray(SECTION_FACTORS)[:, None, None] * np.kron(np.eye(NV), matrix)
    matrix = matrix.astype(np.float32)
    lead = matrix.astype(ml_dtypes.bfloat16)
    rest = (matrix - lead.astype(np.float32)).astype(ml_dtypes.bfloat16)
    return np.concatenate([lead, rest, lead], axis=2)


def params(mib):
    return pltpu.CompilerParams(vmem_limit_bytes=mib << 20)


def place():
    return lax.axis_index("tm"), lax.axis_index("block")


def pack_kernel(state_in, far_in, index_in, weight_in, out, state, far, index, weight, sems):
    copies = [
        pltpu.make_async_copy(source, target, sems.at[i])
        for i, (source, target) in enumerate(
            ((state_in, state), (far_in, far), (index_in, index), (weight_in, weight))
        )
    ]
    for copy in copies:
        copy.start()
    for copy in copies:
        copy.wait()
    _, block = place()

    def fill(rotor):
        for t in range(PARTS):
            first = t * CHUNK if rotor else 256 - (t + 1) * CHUNK
            skip = max(-first, 0)
            count = min(CHUNK, 256 - first) - skip
            for v in range(NV):
                at = v * ROW + skip
                out[t, at : at + count] = state[v, first + skip : first + skip + count]
                out[t, v * ROW + CHUNK : (v + 1) * ROW] = far[v : v + 1]
        lines = []
        for line in range(HALO):
            cell = 255 - line if rotor else line
            lines += [state[v, cell : cell + 1] for v in range(NV)]
        lines += [index[...].astype(jnp.float32)] + [weight[k : k + 1] for k in range(4)]
        for t, half in ((PARTS, FIRST_HALF), (PARTS + 1, SECOND_HALF)):
            for i, k in enumerate(half):
                out[t, i : i + 1] = lines[k]

    @pl.when(block < HALF)
    def _():
        fill(True)

    @pl.when(block >= HALF)
    def _():
        fill(False)


def line_address(side, r, v):
    return v * ROW + jnp.where(side == 0, r, CHUNK - 1 - r)


def zone_kernel(lines, zone, ends_up, ends_down):
    _, block = place()
    side = block // HALF
    for i in range(HALF_ZONE):
        tile = lines[pl.ds(i, NT, stride=NR), :]
        for b in range(BLOCKS):
            zone[b, i * NT : (i + 1) * NT] = tile
    for i in range(ENDS):
        r, v = i // NV, i % NV
        at = slice(i * NT, (i + 1) * NT)
        ends_up[at] = lines[pl.ds(line_address(side, CHUNK - HALO + r, v), NT, stride=NR), :]
        ends_down[at] = lines[pl.ds(line_address(side, r, v), NT, stride=NR), :]


def line_tile(lines, below, above, t, side, r, v):
    if r < 0:
        at = (r + HALO) * NV + v
        tile = below[at * NT : (at + 1) * NT]
        if r == -1:
            tile = jnp.where(t == 0, lines[pl.ds(v * ROW + CHUNK, NT, stride=NR), :], tile)
        return tile
    if r < CHUNK:
        return lines[pl.ds(line_address(side, r, v), NT, stride=NR), :]
    at = (r - CHUNK) * NV + v
    return above[at * NT : (at + 1) * NT]


def edge_kernel(lines, below, above, left, right):
    t, block = place()
    side = block // HALF
    part = lax.broadcasted_iota(jnp.int32, (NT, W), 1) // 8
    for p in range(EDGE_PACKS):
        left_pack = jnp.zeros((NT, W), jnp.float32)
        right_pack = jnp.zeros((NT, W), jnp.float32)
        for k in range(16):
            m = p * 16 + k
            if m >= LINES * NV:
                break
            tile = line_tile(lines, below, above, t, side, m // NV - HALO, m % NV)
            moved = tile if k == 0 else pltpu.roll(tile, 8 * k, 1)
            left_pack = jnp.where(part == k, moved, left_pack)
            moved = tile if k == 15 else pltpu.roll(tile, 8 * k + 8, 1)
            right_pack = jnp.where(part == k, moved, right_pack)
        left[p * NT : (p + 1) * NT] = left_pack
        right[p * NT : (p + 1) * NT] = right_pack


def coefficients(flow, side, factor):
    sign = (0.5, -0.5)[side] if isinstance(side, int) else jnp.where(side == 0, 0.5, -0.5)
    along = sign * flow[side, 0]
    across = 0.5 * flow[side, 1]
    return (
        factor * sign,
        0.5 * factor,
        factor * (along - DISSIPATION),
        factor * (-along - DISSIPATION),
        factor * (across - DISSIPATION),
        factor * (-across - DISSIPATION),
    )


def rates(coefs, up, down, nxt, prv, timed):
    ci, cj, cu, cd, cn, cp = coefs
    plain = [timed[v] + (cu * up[v] + cd * down[v]) + (cn * nxt[v] + cp * prv[v]) for v in range(NV)]
    mixed = ci * (up[1] - down[1]) + cj * (nxt[2] - prv[2])
    pressure_up = ci * (up[3] - down[3])
    pressure_next = cj * (nxt[3] - prv[3])
    return [plain[0] + mixed, plain[1] + pressure_up, plain[2] + pressure_next, plain[3] + mixed]


def level_product(matrix, values):
    lead = values.astype(jnp.bfloat16)
    rest = (values - lead.astype(jnp.float32)).astype(jnp.bfloat16)
    return jnp.dot(matrix, jnp.concatenate([lead, lead, rest], axis=0), preferred_element_type=jnp.float32)


def split(lines):
    return [lines[v * NT : (v + 1) * NT] for v in range(NV)]


def zone_tile(first_half, second_half, side, j, k):
    source, at = (first_half, FIRST_HALF.index(k)) if k in FIRST_HALF else (second_half, SECOND_HALF.index(k))
    return source[HALF * side + j, at * NT : (at + 1) * NT, :]


def start_kernel(high, table, ghosts, ordered):
    def tile(side, j, k):
        return zone_tile(None, high, side, j, k)

    def interpolate_first(side, j):
        first = tile(side, j, 20).astype(jnp.int32)
        parts = []
        for h in range(2):
            at = slice(8 * h, 8 * h + 8)
            totals = [None] * NV
            for k in range(4):
                source = (first[at] + k) & (HALF * W - 1)
                within, which = source & (W - 1), source >> 7
                weight = tile(side, j, 21 + k)[at]
                picked = [None] * NV
                for m in range(HALF):
                    here = which == m
                    for v in range(NV):
                        face = tile(1 - side, m, v)[at]
                        got = jnp.take_along_axis(face, within, axis=1, mode="promise_in_bounds")
                        picked[v] = got if m == 0 else jnp.where(here, got, picked[v])
                totals = [weight * picked[v] if k == 0 else totals[v] + weight * picked[v] for v in range(NV)]
            parts.append(totals)
        return [jnp.concatenate([parts[0][v], parts[1][v]], axis=0) for v in range(NV)]

    def order_weights(side, level):
        rows = lambda k: table[pl.ds(HALF * side * HALF_ZONE * NT + k * NT + level, HALF, stride=HALF_ZONE * NT), :]
        first = rows(0).astype(jnp.int32)
        within, which = first & (W - 1), first >> 7
        weight = [rows(1 + k) for k in range(4)]
        eight = lax.broadcasted_iota(jnp.int32, (HALF, W), 0)
        many = lax.broadcasted_iota(jnp.int32, (W, W), 0)
        spread, chosen = [], []
        for j in range(HALF):
            here = jnp.broadcast_to(which[j : j + 1], (HALF, W)) == eight
            spread.append(
                jnp.concatenate(
                    [jnp.where(here, jnp.broadcast_to(weight[k][j : j + 1], (HALF, W)), 0.0) for k in range(4)], axis=0
                )
            )
            hit = jnp.broadcast_to(within[j : j + 1], (W, W)) == many
            chosen.append(jnp.where(hit, 1.0, 0.0).astype(jnp.bfloat16))
        spread = jnp.concatenate(spread, axis=1)
        chosen = jnp.concatenate(chosen, axis=1)
        lead = spread.astype(jnp.bfloat16)
        rest = (spread - lead.astype(jnp.float32)).astype(jnp.bfloat16)
        both = lax.dot_general(
            jnp.concatenate([lead, rest], axis=0), chosen, (((1,), (1,)), ((), ())), preferred_element_type=jnp.float32
        )
        both = both[:32] + both[32:]
        for k in range(4):
            ordered[side, k, pl.ds(level, HALF, stride=NT), :] = both[8 * k : 8 * k + 8]

    def step(j, _):
        for side in range(2):
            ghost = interpolate_first(side, j)
            for v in range(NV):
                ghosts[side, v, j] = ghost[v]
            order_weights(side, 2 * j)
            order_weights(side, 2 * j + 1)
        return 0

    @pl.when(place()[0] >= PARTS)
    def _():
        lax.fori_loop(0, HALF, step, 0)


def chain(
    low, high, given_ghosts, ordered, matrix, flow, out,
    cur0, cur1, weighed, ghosts, applied,
):
    _, block = place()
    own_side, own = block // HALF, block % HALF
    lane = lax.broadcasted_iota(jnp.int32, (NT, W), 1)
    cur = (cur0, cur1)

    def tile(side, j, k):
        return zone_tile(low, high, side, j, k)

    def value(section, side, line, v, j):
        if section == 0:
            return tile(side, j, line * NV + v)
        return cur[section % 2][side, line, v, j]

    def weigh(section, side, m):
        other, after = 1 - side, (m + 1) % HALF
        weight = [ordered[side, k, pl.ds(pl.multiple_of(m * NT, NT), NT), :] for k in range(4)]
        for v in range(NV):
            total = weight[0] * value(section, other, 0, v, m)
            for k in range(1, 4):
                ahead = jnp.where(lane < k, value(section, other, 0, v, after), value(section, other, 0, v, m))
                total = total + weight[k] * pltpu.roll(ahead, W - k, 1)
            weighed[side, v, m] = total

    def interpolate(side, j):
        first = tile(side, j, 20).astype(jnp.int32)
        within, which = first & (W - 1), first >> 7
        parts = []
        for h in range(2):
            at = slice(8 * h, 8 * h + 8)
            picked = [None] * NV
            for m in range(HALF):
                here = which[at] == m
                for v in range(NV):
                    got = jnp.take_along_axis(weighed[side, v, m, at], within[at], axis=1, mode="promise_in_bounds")
                    picked[v] = got if m == 0 else jnp.where(here, got, picked[v])
            parts.append(picked)
        return [jnp.concatenate([parts[0][v], parts[1][v]], axis=0) for v in range(NV)]

    for s in range(4):
        sides = (0, 1) if s < 3 else (1 - own_side,)

        def weigh_step(m, _, s=s):
            weigh(s, 0, m)
            weigh(s, 1, m)
            return 0

        def advance(side, j, s=s):
            after, before = (j + 1) % HALF, (j + HALF - 1) % HALF
            coefs = coefficients(flow, side, SECTION_FACTORS[s])
            if s == 0:
                ghost = [given_ghosts[side, v, j] for v in range(NV)]
            else:
                ghost = interpolate(side, j)
                for v in range(NV):
                    ghosts[s % 2, side, v, j] = ghost[v]
            lines = 4 - s
            here = [[value(s, side, line, v, j) for v in range(NV)] for line in range(lines + 1)]
            product = level_product(
                matrix[s], jnp.concatenate([jnp.concatenate(here[line], axis=0) for line in range(lines)], axis=1)
            )
            for line in reversed(range(lines)):
                up = ghost if line == 0 else here[line - 1]
                nxt, prv = [], []
                for v in range(NV):
                    ahead = jnp.where(lane == 0, value(s, side, line, v, after), here[line][v])
                    behind = jnp.where(lane == W - 1, value(s, side, line, v, before), here[line][v])
                    nxt.append(pltpu.roll(ahead, W - 1, 1))
                    prv.append(pltpu.roll(behind, 1, 1))
                timed = split(product[:, line * W : (line + 1) * W])
                rate = rates(coefs, up, here[line + 1], nxt, prv, timed)
                for v in range(NV):
                    result = value(0, side, line, v, j) - rate[v]
                    cur[(s + 1) % 2][side, line, v, j] = result
        def section_step(j, _, advance=advance, sides=sides):
            for side in sides:
                advance(side, j)
            return 0

        if s > 0:
            lax.fori_loop(0, HALF, weigh_step, 0, unroll=8)
        lax.fori_loop(0, HALF, section_step, 0, unroll=SU[s])
        if s == 3:

            def own_step(step, _):
                j = (own + HALF - 1 + step) % HALF
                ghost = interpolate(own_side, j)
                for v in range(NV):
                    ghosts[1, own_side, v, j] = ghost[v]
                return 0

            lax.fori_loop(0, 3, own_step, 0, unroll=3)
        kept = given_ghosts if s == 0 else ghosts.at[s % 2]
        for v in range(NV):
            at = slice(v * NT, (v + 1) * NT)
            applied[s, at, :W] = kept[own_side, v, own]
            after = kept[own_side, v, (own + 1) % HALF]
            before = kept[own_side, v, (own + HALF - 1) % HALF]
            applied[s, at, W:] = jnp.where(lane < W // 2, after, before)

    def last_weigh(m, _):
        weigh(4, own_side, m)
        return 0

    lax.fori_loop(0, HALF, last_weigh, 0, unroll=8)
    got = interpolate(own_side, own)
    for v in range(NV):
        at = slice(v * NT, (v + 1) * NT)
        applied[4, at, :W] = got[v]
        applied[4, at, W:] = got[v]

    zero = jnp.zeros((NV * NT, 2 * W), jnp.float32)
    response = []
    for s in range(5):
        coefs = coefficients(flow, own_side, SECTION_FACTORS[s])
        product = None
        if s:
            product = level_product(matrix[s], jnp.concatenate(response, axis=1))
        padded = [applied[s]] + response + [zero, zero]
        new = []
        for line in range(s + 1):
            here = padded[line + 1]
            if line < s:
                nxt, prv = pltpu.roll(here, 2 * W - 1, 1), pltpu.roll(here, 1, 1)
                timed = product[:, 2 * W * line : 2 * W * (line + 1)]
            else:
                nxt = prv = timed = zero
            rate = rates(coefs, split(padded[line]), split(padded[line + 2]), split(nxt), split(prv), split(timed))
            new.append(-jnp.concatenate(rate, axis=0))
        response = new

    for line in range(HALO):
        for v in range(NV):
            cell = jnp.where(own_side == 0, HALO - 1 - line, line)
            out[pl.ds(v * ROW + cell, NT, stride=NR), :] = response[line][v * NT : (v + 1) * NT, :W]


def bulk(lines, below, above, from_left, from_right, matrix, flow, out, start, even, odd):
    t, block = place()
    side = block // HALF
    lane = lax.broadcasted_iota(jnp.int32, (NT, W), 1)
    for m in range(LINES * NV):
        r, v = m // NV - HALO, m % NV
        at = slice(v * NT, (v + 1) * NT)
        start[m // NV, at, :W] = line_tile(lines, below, above, t, side, r, v)
        p, k = m // 16, m % 16
        after = from_right[p * NT : (p + 1) * NT]
        after = after if k == 0 else pltpu.roll(after, W - 8 * k, 1)
        before = from_left[p * NT : (p + 1) * NT]
        before = before if k == 15 else pltpu.roll(before, 120 - 8 * k, 1)
        start[m // NV, at, W:] = jnp.where(lane < W // 2, after, before)
    group = 4
    for s in range(5):
        coefs = coefficients(flow, side, SECTION_FACTORS[s])
        now = start if s == 0 else (even if s % 2 == 0 else odd)
        new = odd if s % 2 == 0 else even

        @pl.when(t == PARTS - 1)
        def _(now=now):
            now[HALO + TAIL] = jnp.zeros((NV * NT, 2 * W), jnp.float32)

        if s > 0:

            @pl.when(t == 0)
            def _(now=now):
                now[HALO - 1] = start[HALO - 1]

        first = (1, 1, 3, 3, 5)[s]

        def line_step(step, _, now=now, new=new, s=s, first=first, coefs=coefs):
            i = first + group * step
            here = [now[i - 1 + g] for g in range(group + 2)]
            product = level_product(matrix[s], jnp.concatenate(here[1:-1], axis=1))
            for g in range(group):
                line = here[g + 1]
                nxt = pltpu.roll(line, 2 * W - 1, 1)
                prv = pltpu.roll(line, 1, 1)
                timed = split(product[:, 2 * W * g : 2 * W * (g + 1)])
                rate = rates(coefs, split(here[g + 2]), split(here[g]), split(nxt), split(prv), timed)
                base = split(start[i + g])
                for v in range(NV):
                    result = base[v] - rate[v]
                    if s < 4:
                        new[i + g, v * NT : (v + 1) * NT] = result
                    else:
                        cell = jnp.where(side == 0, i + g - HALO, CHUNK + HALO - i - g)
                        out[pl.ds(v * ROW + cell, NT, stride=NR), :] = result[:, :W]
            return 0

        lax.fori_loop(0, (LINES - 2 * first + group - 1) // group, line_step, 0)


def main_kernel(
    low, high, given_ghosts, ordered, lines, below, above, from_left, from_right, matrix, flow, out, *scratch
):
    t, _ = place()

    @pl.when(t < PARTS)
    def _():
        bulk(lines, below, above, from_left, from_right, matrix, flow, out, *scratch[:3])

    @pl.when(t >= PARTS)
    def _():
        chain(low, high, given_ghosts, ordered, matrix, flow, out, *scratch[3:])


def unpack_kernel(shares, out):
    _, block = place()

    def fill(rotor):
        for t in range(PARTS):
            first = t * CHUNK if rotor else 256 - (t + 1) * CHUNK
            skip = max(-first, 0)
            count = min(CHUNK, 256 - first) - skip
            for v in range(NV):
                at = v * ROW + skip + (0 if rotor else 1)
                share = shares[t, at : at + count]
                if t == PARTS - 1:
                    added = shares[NT - 1, v * ROW : v * ROW + HALO]
                    none = jnp.zeros((count - HALO, W), jnp.float32)
                    share = share + jnp.concatenate([none, added] if rotor else [added, none], axis=0)
                out[v, first + skip : first + skip + count] = share

    @pl.when(block < HALF)
    def _():
        fill(True)

    @pl.when(block >= HALF)
    def _():
        fill(False)


def f32(*shape):
    return jax.ShapeDtypeStruct(shape, jnp.float32)


def cost(flops, nbytes):
    return pl.CostEstimate(flops=flops, bytes_accessed=nbytes, transcendentals=0)


def shards(state, far_field, face_index, face_weight, mean_flow):
    matrix = jnp.asarray(level_matrix())
    shares = pl.pallas_call(
        pack_kernel,
        out_shape=f32(NT, NR, W),
        in_specs=[HBM] * 4,
        out_specs=VMEM,
        scratch_shapes=[
            pltpu.VMEM((NV, 256, W), jnp.float32),
            pltpu.VMEM((NV, W), jnp.float32),
            pltpu.VMEM((1, W), jnp.int32),
            pltpu.VMEM((NV, W), jnp.float32),
            pltpu.SemaphoreType.DMA((4,)),
        ],
        compiler_params=params(60),
        name="pack",
    )(state[0], far_field[0], face_index, face_weight[0])
    lines = lax.all_to_all(shares, "tm", 0, 0, tiled=True).reshape(NT * NR, W)
    zone, ends_up, ends_down = pl.pallas_call(
        zone_kernel,
        out_shape=[f32(BLOCKS, HALF_ZONE * NT, W)] + [f32(ENDS * NT, W)] * 2,
        in_specs=[VMEM],
        out_specs=[VMEM] * 3,
        compiler_params=params(16),
        name="zone",
    )(lines)
    high = lax.all_to_all(zone, "block", 0, 0, tiled=True)
    below = lax.ppermute(ends_up, "tm", [(i, i + 1) for i in range(PARTS - 1)])
    above = lax.ppermute(ends_down, "tm", [(i + 1, i) for i in range(PARTS - 1)])
    left, right = pl.pallas_call(
        edge_kernel,
        out_shape=[f32(EDGE_PACKS * NT, W)] * 2,
        in_specs=[VMEM] * 3,
        out_specs=[VMEM] * 2,
        compiler_params=params(16),
        name="edges",
    )(lines, below, above)
    rights = [
        (i * BLOCKS + b, i * BLOCKS + b // HALF * HALF + (b + 1) % HALF) for i in range(PARTS) for b in range(BLOCKS)
    ]
    from_left = lax.ppermute(right, ("tm", "block"), rights)
    from_right = lax.ppermute(left, ("tm", "block"), [(b, a) for a, b in rights])
    high, from_left, from_right = lax.optimization_barrier((high, from_left, from_right))
    low = lax.ppermute(high, "tm", [(PARTS, PARTS + 1)])
    given_ghosts, ordered = pl.pallas_call(
        start_kernel,
        out_shape=[f32(2, NV, HALF, NT, W), f32(2, 4, HALF * NT, W)],
        in_specs=[VMEM] * 2,
        out_specs=[VMEM] * 2,
        compiler_params=params(16),
        cost_estimate=cost(4 * 10**9, 16 << 20),
        name="start",
    )(high, high.reshape(BLOCKS * HALF_ZONE * NT, W))
    grid = pltpu.VMEM((LINES + 3, NV * NT, 2 * W), jnp.float32)
    lines_of = pltpu.VMEM((2, 4, NV, HALF, NT, W), jnp.float32)
    faces_of = pltpu.VMEM((2, 2, NV, HALF, NT, W), jnp.float32)
    done = pl.pallas_call(
        main_kernel,
        out_shape=f32(NT * NR, W),
        in_specs=[VMEM] * 10 + [SMEM],
        out_specs=VMEM,
        scratch_shapes=[grid] * 3
        + [lines_of] * 2
        + [pltpu.VMEM((2, NV, HALF, NT, W), jnp.float32)]
        + [faces_of, pltpu.VMEM((5, NV * NT, 2 * W), jnp.float32)],
        compiler_params=params(32),
        cost_estimate=cost(8 * 10**9, 64 << 20),
        name="main",
    )(low, high, given_ghosts, ordered, lines, below, above, from_left, from_right, matrix, mean_flow)
    done = lax.all_to_all(done.reshape(NT, NR, W), "tm", 0, 0, tiled=True)
    result = pl.pallas_call(
        unpack_kernel,
        out_shape=f32(NV, 256, W),
        in_specs=[VMEM],
        out_specs=VMEM,
        compiler_params=params(16),
        name="unpack",
    )(done)
    return result[None]


def solution(mesh):
    in_specs = (
        P("tm", None, None, "block"),
        P("tm", None, "block"),
        P("tm", "block"),
        P("tm", None, "block"),
        P(),
    )
    out_specs = P("tm", None, None, "block")
    return jax.shard_map(shards, mesh=mesh, in_specs=in_specs, out_specs=out_specs, check_vma=False)
```

```python
import jax
import jax.numpy as jnp
import ml_dtypes
import numpy as np
from jax import lax
from jax.experimental import pallas as pl
from jax.experimental.pallas import tpu as pltpu
from jax.sharding import PartitionSpec as P

SECTION_FACTORS = (0.075, 0.05, 0.1125, 0.15, 0.3)
OMEGA = 1.0
DISSIPATION = 0.2

NT = 16
NV = 4
PARTS = 14
CHUNK = 19
HALO = 5
LINES = CHUNK + 2 * HALO
TAIL = 256 - (PARTS - 1) * CHUNK
W = 128
HALF = 8
BLOCKS = 16
NR = 80
ROW = 20
HALF_ZONE = 13
ENDS = HALO * NV
EDGE_PACKS = 8
FIRST_HALF = tuple(range(4, 17))
SECOND_HALF = (20, 21, 22, 23, 24, 0, 1, 2, 3, 17, 18, 19)
SU = (2, 4, 4, 8)
VMEM = pl.BlockSpec(memory_space=pltpu.VMEM)
HBM = pl.BlockSpec(memory_space=pltpu.HBM)
SMEM = pl.BlockSpec(memory_space=pltpu.SMEM)


def level_matrix():
    offsets = np.arange(NT)[:, None] - np.arange(NT)[None, :]
    angle = np.pi * offsets / NT
    safe = np.where(offsets == 0, 0.5 * np.pi, angle)
    cot = np.cos(safe) / np.sin(safe)
    matrix = np.where(offsets == 0, 0.0, 0.5 * (1.0 - 2.0 * (offsets % 2)) * cot)
    matrix = OMEGA * matrix + 4.0 * DISSIPATION * np.eye(NT)
    matrix = np.asarray(SECTION_FACTORS)[:, None, None] * np.kron(np.eye(NV), matrix)
    matrix = matrix.astype(np.float32)
    lead = matrix.astype(ml_dtypes.bfloat16)
    rest = (matrix - lead.astype(np.float32)).astype(ml_dtypes.bfloat16)
    return np.concatenate([lead, rest, lead], axis=2)


def params(mib):
    return pltpu.CompilerParams(vmem_limit_bytes=mib << 20)


def place():
    return lax.axis_index("tm"), lax.axis_index("block")


def pack_kernel(state_in, far_in, index_in, weight_in, out, state, far, index, weight, sems):
    copies = [
        pltpu.make_async_copy(source, target, sems.at[i])
        for i, (source, target) in enumerate(
            ((state_in, state), (far_in, far), (index_in, index), (weight_in, weight))
        )
    ]
    for copy in copies:
        copy.start()
    for copy in copies:
        copy.wait()
    _, block = place()

    def fill(rotor):
        for t in range(PARTS):
            first = t * CHUNK if rotor else 256 - (t + 1) * CHUNK
            skip = max(-first, 0)
            count = min(CHUNK, 256 - first) - skip
            for v in range(NV):
                at = v * ROW + skip
                out[t, at : at + count] = state[v, first + skip : first + skip + count]
                out[t, v * ROW + CHUNK : (v + 1) * ROW] = far[v : v + 1]
        lines = []
        for line in range(HALO):
            cell = 255 - line if rotor else line
            lines += [state[v, cell : cell + 1] for v in range(NV)]
        lines += [index[...].astype(jnp.float32)] + [weight[k : k + 1] for k in range(4)]
        for t, half in ((PARTS, FIRST_HALF), (PARTS + 1, SECOND_HALF)):
            for i, k in enumerate(half):
                out[t, i : i + 1] = lines[k]

    @pl.when(block < HALF)
    def _():
        fill(True)

    @pl.when(block >= HALF)
    def _():
        fill(False)


def line_address(side, r, v):
    return v * ROW + jnp.where(side == 0, r, CHUNK - 1 - r)


def ends_kernel(lines, to_partner, to_chip):
    t, block = place()
    side = block // HALF
    even = t % 2 == 0
    for i in range(ENDS):
        r, v = i // NV, i % NV
        at = slice(i * NT, (i + 1) * NT)
        up = lines[pl.ds(line_address(side, CHUNK - HALO + r, v), NT, stride=NR), :]
        down = lines[pl.ds(line_address(side, r, v), NT, stride=NR), :]
        to_partner[at] = jnp.where(even, up, down)
        to_chip[at] = jnp.where(even, down, up)


def neighbours(block):
    row = block // HALF * HALF
    return row + (block + HALF - 1) % HALF, row + (block + 1) % HALF


def line_tile(lines, partner, chip, t, side, r, v):
    even = t % 2 == 0
    if 0 <= r < CHUNK:
        return lines[pl.ds(line_address(side, r, v), NT, stride=NR), :]
    at = (r + HALO if r < 0 else r - CHUNK) * NV + v
    at = slice(at * NT, (at + 1) * NT)
    if r >= CHUNK:
        return jnp.where(even, partner[at], chip[at])
    tile = jnp.where(even, chip[at], partner[at])
    if r == -1:
        tile = jnp.where(t == 0, lines[pl.ds(v * ROW + CHUNK, NT, stride=NR), :], tile)
    return tile


def zone_kernel(lines, from_partner, from_chip, zone):
    t, block = place()
    side = block // HALF
    before, after = neighbours(block)
    part = lax.broadcasted_iota(jnp.int32, (NT, W), 1) // 8

    @pl.when(t >= PARTS)
    def _():
        for i in range(HALF_ZONE):
            tile = lines[pl.ds(i, NT, stride=NR), :]
            for b in range(BLOCKS):
                zone[b, i * NT : (i + 1) * NT] = tile

    @pl.when(t < PARTS)
    def _():
        for p in range(EDGE_PACKS):
            left_pack = jnp.zeros((NT, W), jnp.float32)
            right_pack = jnp.zeros((NT, W), jnp.float32)
            for k in range(16):
                m = p * 16 + k
                if m >= LINES * NV:
                    break
                tile = line_tile(lines, from_partner, from_chip, t, side, m // NV - HALO, m % NV)
                moved = tile if k == 0 else pltpu.roll(tile, 8 * k, 1)
                left_pack = jnp.where(part == k, moved, left_pack)
                moved = tile if k == 15 else pltpu.roll(tile, 8 * k + 8, 1)
                right_pack = jnp.where(part == k, moved, right_pack)
            zone[before, p * NT : (p + 1) * NT] = left_pack
            zone[after, p * NT : (p + 1) * NT] = right_pack


def coefficients(flow, side, factor):
    sign = (0.5, -0.5)[side] if isinstance(side, int) else jnp.where(side == 0, 0.5, -0.5)
    along = sign * flow[side, 0]
    across = 0.5 * flow[side, 1]
    return (
        factor * sign,
        0.5 * factor,
        factor * (along - DISSIPATION),
        factor * (-along - DISSIPATION),
        factor * (across - DISSIPATION),
        factor * (-across - DISSIPATION),
    )


def rates(coefs, up, down, nxt, prv, timed):
    ci, cj, cu, cd, cn, cp = coefs
    plain = [timed[v] + (cu * up[v] + cd * down[v]) + (cn * nxt[v] + cp * prv[v]) for v in range(NV)]
    mixed = ci * (up[1] - down[1]) + cj * (nxt[2] - prv[2])
    pressure_up = ci * (up[3] - down[3])
    pressure_next = cj * (nxt[3] - prv[3])
    return [plain[0] + mixed, plain[1] + pressure_up, plain[2] + pressure_next, plain[3] + mixed]


def level_product(matrix, values):
    lead = values.astype(jnp.bfloat16)
    rest = (values - lead.astype(jnp.float32)).astype(jnp.bfloat16)
    return jnp.dot(matrix, jnp.concatenate([lead, lead, rest], axis=0), preferred_element_type=jnp.float32)


def split(lines):
    return [lines[v * NT : (v + 1) * NT] for v in range(NV)]


def zone_tile(first_half, second_half, side, j, k):
    source, at = (first_half, FIRST_HALF.index(k)) if k in FIRST_HALF else (second_half, SECOND_HALF.index(k))
    return source[HALF * side + j, at * NT : (at + 1) * NT, :]


def start_kernel(high, table, ghosts, ordered):
    def tile(side, j, k):
        return zone_tile(None, high, side, j, k)

    def interpolate_first(side, j):
        first = tile(side, j, 20).astype(jnp.int32)
        parts = []
        for h in range(2):
            at = slice(8 * h, 8 * h + 8)
            totals = [None] * NV
            for k in range(4):
                source = (first[at] + k) & (HALF * W - 1)
                within, which = source & (W - 1), source >> 7
                weight = tile(side, j, 21 + k)[at]
                picked = [None] * NV
                for m in range(HALF):
                    here = which == m
                    for v in range(NV):
                        face = tile(1 - side, m, v)[at]
                        got = jnp.take_along_axis(face, within, axis=1, mode="promise_in_bounds")
                        picked[v] = got if m == 0 else jnp.where(here, got, picked[v])
                totals = [weight * picked[v] if k == 0 else totals[v] + weight * picked[v] for v in range(NV)]
            parts.append(totals)
        return [jnp.concatenate([parts[0][v], parts[1][v]], axis=0) for v in range(NV)]

    def order_weights(side, level):
        rows = lambda k: table[pl.ds(HALF * side * HALF_ZONE * NT + k * NT + level, HALF, stride=HALF_ZONE * NT), :]
        first = rows(0).astype(jnp.int32)
        within, which = first & (W - 1), first >> 7
        weight = [rows(1 + k) for k in range(4)]
        eight = lax.broadcasted_iota(jnp.int32, (HALF, W), 0)
        many = lax.broadcasted_iota(jnp.int32, (W, W), 0)
        spread, chosen = [], []
        for j in range(HALF):
            here = jnp.broadcast_to(which[j : j + 1], (HALF, W)) == eight
            spread.append(
                jnp.concatenate(
                    [jnp.where(here, jnp.broadcast_to(weight[k][j : j + 1], (HALF, W)), 0.0) for k in range(4)], axis=0
                )
            )
            hit = jnp.broadcast_to(within[j : j + 1], (W, W)) == many
            chosen.append(jnp.where(hit, 1.0, 0.0).astype(jnp.bfloat16))
        spread = jnp.concatenate(spread, axis=1)
        chosen = jnp.concatenate(chosen, axis=1)
        lead = spread.astype(jnp.bfloat16)
        rest = (spread - lead.astype(jnp.float32)).astype(jnp.bfloat16)
        both = lax.dot_general(
            jnp.concatenate([lead, rest], axis=0), chosen, (((1,), (1,)), ((), ())), preferred_element_type=jnp.float32
        )
        both = both[:32] + both[32:]
        for k in range(4):
            ordered[side, k, pl.ds(level, HALF, stride=NT), :] = both[8 * k : 8 * k + 8]

    def step(j, _):
        for side in range(2):
            ghost = interpolate_first(side, j)
            for v in range(NV):
                ghosts[side, v, j] = ghost[v]
            order_weights(side, 2 * j)
            order_weights(side, 2 * j + 1)
        return 0

    @pl.when(place()[0] >= PARTS)
    def _():
        lax.fori_loop(0, HALF, step, 0)


def chain(
    low, high, given_ghosts, ordered, matrix, flow, out,
    cur0, cur1, weighed, ghosts, applied,
):
    _, block = place()
    own_side, own = block // HALF, block % HALF
    lane = lax.broadcasted_iota(jnp.int32, (NT, W), 1)
    cur = (cur0, cur1)

    def tile(side, j, k):
        return zone_tile(low, high, side, j, k)

    def value(section, side, line, v, j):
        if section == 0:
            return tile(side, j, line * NV + v)
        return cur[section % 2][side, line, v, j]

    def weigh(section, side, m):
        other, after = 1 - side, (m + 1) % HALF
        weight = [ordered[side, k, pl.ds(pl.multiple_of(m * NT, NT), NT), :] for k in range(4)]
        for v in range(NV):
            total = weight[0] * value(section, other, 0, v, m)
            for k in range(1, 4):
                ahead = jnp.where(lane < k, value(section, other, 0, v, after), value(section, other, 0, v, m))
                total = total + weight[k] * pltpu.roll(ahead, W - k, 1)
            weighed[side, v, m] = total

    def interpolate(side, j):
        first = tile(side, j, 20).astype(jnp.int32)
        within, which = first & (W - 1), first >> 7
        parts = []
        for h in range(2):
            at = slice(8 * h, 8 * h + 8)
            picked = [None] * NV
            for m in range(HALF):
                here = which[at] == m
                for v in range(NV):
                    got = jnp.take_along_axis(weighed[side, v, m, at], within[at], axis=1, mode="promise_in_bounds")
                    picked[v] = got if m == 0 else jnp.where(here, got, picked[v])
            parts.append(picked)
        return [jnp.concatenate([parts[0][v], parts[1][v]], axis=0) for v in range(NV)]

    for s in range(4):
        sides = (0, 1) if s < 3 else (1 - own_side,)

        def weigh_step(m, _, s=s):
            weigh(s, 0, m)
            weigh(s, 1, m)
            return 0

        def advance(side, j, s=s):
            after, before = (j + 1) % HALF, (j + HALF - 1) % HALF
            coefs = coefficients(flow, side, SECTION_FACTORS[s])
            if s == 0:
                ghost = [given_ghosts[side, v, j] for v in range(NV)]
            else:
                ghost = interpolate(side, j)
                for v in range(NV):
                    ghosts[s % 2, side, v, j] = ghost[v]
            lines = 4 - s
            here = [[value(s, side, line, v, j) for v in range(NV)] for line in range(lines + 1)]
            product = level_product(
                matrix[s], jnp.concatenate([jnp.concatenate(here[line], axis=0) for line in range(lines)], axis=1)
            )
            for line in reversed(range(lines)):
                up = ghost if line == 0 else here[line - 1]
                nxt, prv = [], []
                for v in range(NV):
                    ahead = jnp.where(lane == 0, value(s, side, line, v, after), here[line][v])
                    behind = jnp.where(lane == W - 1, value(s, side, line, v, before), here[line][v])
                    nxt.append(pltpu.roll(ahead, W - 1, 1))
                    prv.append(pltpu.roll(behind, 1, 1))
                timed = split(product[:, line * W : (line + 1) * W])
                rate = rates(coefs, up, here[line + 1], nxt, prv, timed)
                for v in range(NV):
                    result = value(0, side, line, v, j) - rate[v]
                    cur[(s + 1) % 2][side, line, v, j] = result
        def section_step(j, _, advance=advance, sides=sides):
            for side in sides:
                advance(side, j)
            return 0

        if s > 0:
            lax.fori_loop(0, HALF, weigh_step, 0, unroll=8)
        lax.fori_loop(0, HALF, section_step, 0, unroll=SU[s])
        if s == 3:

            def own_step(step, _):
                j = (own + HALF - 1 + step) % HALF
                ghost = interpolate(own_side, j)
                for v in range(NV):
                    ghosts[1, own_side, v, j] = ghost[v]
                return 0

            lax.fori_loop(0, 3, own_step, 0, unroll=3)
        kept = given_ghosts if s == 0 else ghosts.at[s % 2]
        for v in range(NV):
            at = slice(v * NT, (v + 1) * NT)
            applied[s, at, :W] = kept[own_side, v, own]
            after = kept[own_side, v, (own + 1) % HALF]
            before = kept[own_side, v, (own + HALF - 1) % HALF]
            applied[s, at, W:] = jnp.where(lane < W // 2, after, before)

    def last_weigh(m, _):
        weigh(4, own_side, m)
        return 0

    lax.fori_loop(0, HALF, last_weigh, 0, unroll=8)
    got = interpolate(own_side, own)
    for v in range(NV):
        at = slice(v * NT, (v + 1) * NT)
        applied[4, at, :W] = got[v]
        applied[4, at, W:] = got[v]

    zero = jnp.zeros((NV * NT, 2 * W), jnp.float32)
    response = []
    for s in range(5):
        coefs = coefficients(flow, own_side, SECTION_FACTORS[s])
        product = None
        if s:
            product = level_product(matrix[s], jnp.concatenate(response, axis=1))
        padded = [applied[s]] + response + [zero, zero]
        new = []
        for line in range(s + 1):
            here = padded[line + 1]
            if line < s:
                nxt, prv = pltpu.roll(here, 2 * W - 1, 1), pltpu.roll(here, 1, 1)
                timed = product[:, 2 * W * line : 2 * W * (line + 1)]
            else:
                nxt = prv = timed = zero
            rate = rates(coefs, split(padded[line]), split(padded[line + 2]), split(nxt), split(prv), split(timed))
            new.append(-jnp.concatenate(rate, axis=0))
        response = new

    for line in range(HALO):
        for v in range(NV):
            cell = jnp.where(own_side == 0, HALO - 1 - line, line)
            out[pl.ds(v * ROW + cell, NT, stride=NR), :] = response[line][v * NT : (v + 1) * NT, :W]


def bulk(lines, from_partner, from_chip, edges, matrix, flow, out, start, even, odd):
    t, block = place()
    side = block // HALF
    left, right = neighbours(block)
    lane = lax.broadcasted_iota(jnp.int32, (NT, W), 1)
    for m in range(LINES * NV):
        r, v = m // NV - HALO, m % NV
        at = slice(v * NT, (v + 1) * NT)
        start[m // NV, at, :W] = line_tile(lines, from_partner, from_chip, t, side, r, v)
        p, k = m // 16, m % 16
        after = edges[right, p * NT : (p + 1) * NT]
        after = after if k == 0 else pltpu.roll(after, W - 8 * k, 1)
        before = edges[left, p * NT : (p + 1) * NT]
        before = before if k == 15 else pltpu.roll(before, 120 - 8 * k, 1)
        start[m // NV, at, W:] = jnp.where(lane < W // 2, after, before)
    group = 4
    for s in range(5):
        coefs = coefficients(flow, side, SECTION_FACTORS[s])
        now = start if s == 0 else (even if s % 2 == 0 else odd)
        new = odd if s % 2 == 0 else even

        @pl.when(t == PARTS - 1)
        def _(now=now):
            now[HALO + TAIL] = jnp.zeros((NV * NT, 2 * W), jnp.float32)

        if s > 0:

            @pl.when(t == 0)
            def _(now=now):
                now[HALO - 1] = start[HALO - 1]

        first = (1, 1, 3, 3, 5)[s]

        def line_step(step, _, now=now, new=new, s=s, first=first, coefs=coefs):
            i = first + group * step
            here = [now[i - 1 + g] for g in range(group + 2)]
            product = level_product(matrix[s], jnp.concatenate(here[1:-1], axis=1))
            for g in range(group):
                line = here[g + 1]
                nxt = pltpu.roll(line, 2 * W - 1, 1)
                prv = pltpu.roll(line, 1, 1)
                timed = split(product[:, 2 * W * g : 2 * W * (g + 1)])
                rate = rates(coefs, split(here[g + 2]), split(here[g]), split(nxt), split(prv), timed)
                base = split(start[i + g])
                for v in range(NV):
                    result = base[v] - rate[v]
                    if s < 4:
                        new[i + g, v * NT : (v + 1) * NT] = result
                    else:
                        cell = jnp.where(side == 0, i + g - HALO, CHUNK + HALO - i - g)
                        out[pl.ds(v * ROW + cell, NT, stride=NR), :] = result[:, :W]
            return 0

        lax.fori_loop(0, (LINES - 2 * first + group - 1) // group, line_step, 0, unroll=True)


def main_kernel(low, high, given_ghosts, ordered, lines, from_partner, from_chip, matrix, flow, out, *scratch):
    t, _ = place()

    @pl.when(t < PARTS)
    def _():
        bulk(lines, from_partner, from_chip, high, matrix, flow, out, *scratch[:3])

    @pl.when(t >= PARTS)
    def _():
        chain(low, high, given_ghosts, ordered, matrix, flow, out, *scratch[3:])


def unpack_kernel(shares, out):
    _, block = place()

    def fill(rotor):
        for t in range(PARTS):
            first = t * CHUNK if rotor else 256 - (t + 1) * CHUNK
            skip = max(-first, 0)
            count = min(CHUNK, 256 - first) - skip
            for v in range(NV):
                at = v * ROW + skip + (0 if rotor else 1)
                share = shares[t, at : at + count]
                if t == PARTS - 1:
                    added = shares[NT - 1, v * ROW : v * ROW + HALO]
                    none = jnp.zeros((count - HALO, W), jnp.float32)
                    share = share + jnp.concatenate([none, added] if rotor else [added, none], axis=0)
                out[v, first + skip : first + skip + count] = share

    @pl.when(block < HALF)
    def _():
        fill(True)

    @pl.when(block >= HALF)
    def _():
        fill(False)


def f32(*shape):
    return jax.ShapeDtypeStruct(shape, jnp.float32)


def cost(flops, nbytes):
    return pl.CostEstimate(flops=flops, bytes_accessed=nbytes, transcendentals=0)


def shards(state, far_field, face_index, face_weight, mean_flow):
    matrix = jnp.asarray(level_matrix())
    shares = pl.pallas_call(
        pack_kernel,
        out_shape=f32(NT, NR, W),
        in_specs=[HBM] * 4,
        out_specs=VMEM,
        scratch_shapes=[
            pltpu.VMEM((NV, 256, W), jnp.float32),
            pltpu.VMEM((NV, W), jnp.float32),
            pltpu.VMEM((1, W), jnp.int32),
            pltpu.VMEM((NV, W), jnp.float32),
            pltpu.SemaphoreType.DMA((4,)),
        ],
        compiler_params=params(60),
        name="pack",
    )(state[0], far_field[0], face_index, face_weight[0])
    lines = lax.all_to_all(shares, "tm", 0, 0, tiled=True).reshape(NT * NR, W)
    to_partner, to_chip = pl.pallas_call(
        ends_kernel,
        out_shape=[f32(ENDS * NT, W)] * 2,
        in_specs=[VMEM],
        out_specs=[VMEM] * 2,
        compiler_params=params(16),
        name="ends",
    )(lines)
    pairs = [(i, i + 1) for i in range(1, PARTS - 1, 2)]
    from_chip = lax.ppermute(to_chip, "tm", pairs + [(b, a) for a, b in pairs])
    from_partner = lax.ppermute(to_partner, "tm", [(i, i ^ 1) for i in range(PARTS)])
    zone = pl.pallas_call(
        zone_kernel,
        out_shape=f32(BLOCKS, HALF_ZONE * NT, W),
        in_specs=[VMEM] * 3,
        out_specs=VMEM,
        compiler_params=params(16),
        name="zone",
    )(lines, from_partner, from_chip)
    high = lax.all_to_all(zone, "block", 0, 0, tiled=True)
    low = lax.ppermute(high, "tm", [(PARTS, PARTS + 1)])
    given_ghosts, ordered = pl.pallas_call(
        start_kernel,
        out_shape=[f32(2, NV, HALF, NT, W), f32(2, 4, HALF * NT, W)],
        in_specs=[VMEM] * 2,
        out_specs=[VMEM] * 2,
        compiler_params=params(16),
        cost_estimate=cost(4 * 10**9, 16 << 20),
        name="start",
    )(high, high.reshape(BLOCKS * HALF_ZONE * NT, W))
    grid = pltpu.VMEM((LINES + 3, NV * NT, 2 * W), jnp.float32)
    lines_of = pltpu.VMEM((2, 4, NV, HALF, NT, W), jnp.float32)
    faces_of = pltpu.VMEM((2, 2, NV, HALF, NT, W), jnp.float32)
    done = pl.pallas_call(
        main_kernel,
        out_shape=f32(NT * NR, W),
        in_specs=[VMEM] * 8 + [SMEM],
        out_specs=VMEM,
        scratch_shapes=[grid] * 3
        + [lines_of] * 2
        + [pltpu.VMEM((2, NV, HALF, NT, W), jnp.float32)]
        + [faces_of, pltpu.VMEM((5, NV * NT, 2 * W), jnp.float32)],
        compiler_params=params(32),
        cost_estimate=cost(8 * 10**9, 64 << 20),
        name="main",
    )(low, high, given_ghosts, ordered, lines, from_partner, from_chip, matrix, mean_flow)
    done = lax.all_to_all(done.reshape(NT, NR, W), "tm", 0, 0, tiled=True)
    result = pl.pallas_call(
        unpack_kernel,
        out_shape=f32(NV, 256, W),
        in_specs=[VMEM],
        out_specs=VMEM,
        compiler_params=params(16),
        name="unpack",
    )(done)
    return result[None]


def solution(mesh):
    in_specs = (
        P("tm", None, None, "block"),
        P("tm", None, "block"),
        P("tm", "block"),
        P("tm", None, "block"),
        P(),
    )
    out_specs = P("tm", None, None, "block")
    return jax.shard_map(shards, mesh=mesh, in_specs=in_specs, out_specs=out_specs, check_vma=False)
```
